32 devices in a mesh: dp: 4 (over y, core), slab: 8 (over z, x).
Axes of the slice: x: 2, y: 2, z: 4, core: 2. Of those that a mesh axis runs over, the one named last changes fastest.
Arguments:
- features: bfloat16 [4, 64, 256, 8, 256], P('dp', None, 'slab'), may hold values from -6 to 6
- target: bfloat16 [4, 256, 8, 256], P('dp', 'slab'), may hold values from -6 to 6
- out_weight: float32 [64], replicated, may hold values from -1.5 to 1.5
- rotation: int32 [4], P('dp'), may hold values from 0 to 3
- blocks: int32 [8, 2], replicated, may hold values from 0 to 3, as said below
- wedge: int32 [256, 256], replicated, may hold values 0 or 1
Outputs:
- vol_grad: float32 [4, 256, 8, 256], P('dp', 'slab')
- w_grad: float32 [64], replicated
The draws below stay inside these ranges and needn't reach their ends.
Inputs may be any that keep to these rules, and one draw needn't show every extreme that they name: `blocks`: the 8 rows are distinct pairs of block indices of the frequency plane, each from 0 to 3.
All inputs are finite; a program needn't handle non-finite values.
Results may differ from the reference program's by a relative error of at most 0.0003.
Values sent between devices are 32-bit elements; how exact they have to be, the bound alone decides.
A program may use at most 64 MiB of HBM per device.

```python
import jax
import jax.numpy as jnp
from jax import lax

C = 64
N = 256
BLK = 64
NB = 8
YP = 8
SAMPLES = 4


def draw_blocks(key, part):
    per_side = N // BLK
    picked = jax.random.permutation(key, per_side * per_side)[:NB]
    return jnp.stack([picked // per_side, picked % per_side], axis=1).astype(jnp.int32)


def place_ends(drawn, stream_key, smallest, top_value):
    longest = drawn.shape.index(max(drawn.shape))
    spots = []
    for shift in (0, 1):
        where = [jax.random.randint(jax.random.fold_in(stream_key, axis), (), 0, length) for axis, length in enumerate(drawn.shape)]
        where[longest] = (where[longest] + shift) % drawn.shape[longest]
        spots.append(tuple(where))
    return drawn.at[spots[0]].set(smallest).at[spots[1]].set(top_value)


def steps_of(own_key, extent, split, low, largest):
    factor_of = 1.0
    for dim, shards_of in split:
        heights = jax.random.uniform(jax.random.fold_in(jax.random.fold_in(own_key, 6), dim), (shards_of,), jnp.float32, low / len(split), largest / len(split))
        factor_of = factor_of * jnp.repeat(jnp.exp(heights), extent[dim] // shards_of).reshape((-1,) + (1,) * (len(extent) - 1 - dim))
    return factor_of


def centred(own_key, dims, deviation, most, cuts=(), kind=jnp.bfloat16):
    values = deviation * jax.random.normal(own_key, dims, jnp.float32)
    if cuts:
        values = values * steps_of(own_key, dims, cuts, -0.22, 0.18)
    return jnp.clip(values, -most, most).astype(kind)


def setup_inputs(seed: int = 0) -> dict:
    streams_of = jax.random.split(jax.random.key(seed), 7)
    return {
        "features": centred(streams_of[0], (SAMPLES, C, N, YP, N), 1.0, 6.0, ((0, 4), (2, 8))),
        "target": centred(streams_of[1], (SAMPLES, N, YP, N), 1.0, 6.0, ((0, 4), (1, 8))),
        "out_weight": centred(streams_of[2], (C,), 0.25, 1.5, (), jnp.float32),
        "rotation": place_ends(jax.random.randint(streams_of[3], (SAMPLES,), 0, 4), jax.random.fold_in(streams_of[3], 1), 0, 3).astype(jnp.int32),
        "blocks": draw_blocks(jax.random.fold_in(streams_of[6], 71), 0),
        "wedge": place_ends((jax.random.randint(streams_of[5], (N, N), 0, 5) < 3).astype(jnp.int32), jax.random.fold_in(streams_of[5], 1), 0, 1),
    }


def turned(volume, turns):
    result = volume
    for count in range(1, 4):
        result = jnp.where(turns == count, jnp.rot90(volume, count, axes=(0, 2)), result)
    return result


def wedge_weights(blocks, wedge):
    per_side = N // BLK
    labels = jnp.arange(per_side, dtype=jnp.int32)
    match = (blocks[:, 0][:, None, None] == labels[None, :, None]) & (blocks[:, 1][:, None, None] == labels[None, None, :])
    listed = jnp.any(match, axis=0)
    spread = jnp.repeat(jnp.repeat(listed, BLK, axis=0), BLK, axis=1)
    return jnp.where(spread, wedge, 0).astype(jnp.float32)


def reference(features, target, out_weight, rotation, blocks, wedge):
    mask = wedge_weights(blocks, wedge)

    def single(items):
        sample, other, turns = items
        wide = sample.astype(jnp.float32)
        volume = jnp.einsum("c,czyx->zyx", out_weight, wide, precision=lax.Precision.HIGHEST)
        difference = volume - other.astype(jnp.float32)
        rotated = turned(difference, turns)
        spectrum = jnp.fft.fft2(rotated, axes=(0, 2)) / N
        grad_spectrum = 2.0 * mask[:, None, :] * spectrum
        rot_grad = N * jnp.real(jnp.fft.ifft2(grad_spectrum, axes=(0, 2)))
        back = turned(rot_grad, (4 - turns) % 4).astype(jnp.float32)
        piece = jnp.einsum("czyx,zyx->c", wide, back, precision=lax.Precision.HIGHEST)
        return back, piece.astype(jnp.float32)

    vol_grad, pieces = lax.map(single, (features, target, rotation))
    w_grad = jnp.sum(pieces, axis=0) / (SAMPLES * N * YP * N)
    return vol_grad, w_grad
```

```python
import functools
import math

import numpy as np

import jax
import jax.numpy as jnp
from jax import lax
from jax.experimental import pallas as pl
from jax.experimental.pallas import tpu as pltpu
from jax.sharding import PartitionSpec as P

BLK = 64
ROWS = 8
OUT_GROUP = 4
BACK_GROUPS = (4, 1)
MESH = pl.DeviceIdType.MESH


def product(form, left, right):
    return jnp.einsum(form, left, right, precision=lax.Precision.HIGHEST)


def wedge_weights(blocks, wedge, length):
    per_side = length // BLK
    labels = jnp.arange(per_side, dtype=jnp.int32)
    match = (blocks[:, 0][:, None, None] == labels[None, :, None]) & (
        blocks[:, 1][:, None, None] == labels[None, None, :]
    )
    listed = jnp.any(match, axis=0)
    spread = jnp.repeat(jnp.repeat(listed, BLK, axis=0), BLK, axis=1)
    return jnp.where(spread, wedge, 0).astype(jnp.float32)


def phase_tables(turns, length):
    positions = jnp.arange(length, dtype=jnp.int32)
    flip_depth = turns >= 2
    flip_width = (turns == 1) | (turns == 2)
    depth_index = jnp.where(
        flip_depth[:, None], length - 1 - positions[None, :], positions[None, :]
    )
    width_index = jnp.where(
        flip_width[:, None], length - 1 - positions[None, :], positions[None, :]
    )
    depth_phase = positions[None, :, None] * depth_index[:, None, :] % length
    width_phase = width_index[:, :, None] * positions[None, None, :] % length
    depth_angle = depth_phase.astype(jnp.float32) * (2.0 * math.pi / length)
    width_angle = width_phase.astype(jnp.float32) * (2.0 * math.pi / length)
    return (jnp.cos(depth_angle), jnp.sin(depth_angle), jnp.cos(width_angle), jnp.sin(width_angle))


def split_lines(features, target, out_weight, rotation, blocks, wedge):
    length = features.shape[-1]
    plane_count = features.shape[3]
    slab_count = lax.axis_size("slab")
    columns = length // slab_count
    col_start = lax.axis_index("slab") * columns
    features_wide = features.astype(jnp.float32)
    volume = product("c,sczyx->szyx", out_weight, features_wide)
    difference = volume - target.astype(jnp.float32)
    depth_cos, depth_sin, width_cos, width_sin = phase_tables(rotation, length)
    line_real = product("szyb,sbp->szyp", difference, width_cos)
    line_imag = -product("szyb,sbp->szyp", difference, width_sin)
    line_real, line_imag = (
        lax.all_to_all(line_real, "slab", split_axis=3, concat_axis=1, tiled=True),
        lax.all_to_all(line_imag, "slab", split_axis=3, concat_axis=1, tiled=True),
    )
    spec_real = (
        product("spa,sayq->spyq", depth_cos, line_real)
        + product("spa,sayq->spyq", depth_sin, line_imag)
    ) / length
    spec_imag = (
        product("spa,sayq->spyq", depth_cos, line_imag)
        - product("spa,sayq->spyq", depth_sin, line_real)
    ) / length
    mask = wedge_weights(blocks, wedge, length)
    odd_turn = rotation % 2 == 1
    mask_turned = jnp.where(odd_turn[:, None, None], mask.T[None], mask[None])
    mask_columns = lax.dynamic_slice_in_dim(mask_turned, col_start, columns, 2)
    grad_real = 2.0 * mask_columns[:, :, None, :] * spec_real
    grad_imag = 2.0 * mask_columns[:, :, None, :] * spec_imag
    back_real = product("spa,spyq->sayq", depth_cos, grad_real) - product(
        "spa,spyq->sayq", depth_sin, grad_imag
    )
    back_imag = product("spa,spyq->sayq", depth_cos, grad_imag) + product(
        "spa,spyq->sayq", depth_sin, grad_real
    )
    back_real, back_imag = (
        lax.all_to_all(back_real, "slab", split_axis=1, concat_axis=3, tiled=True),
        lax.all_to_all(back_imag, "slab", split_axis=1, concat_axis=3, tiled=True),
    )
    vol_grad = (
        product("sayp,sbp->sayb", back_real, width_cos)
        - product("sayp,sbp->sayb", back_imag, width_sin)
    ) / length
    voxel_count = lax.axis_size("dp") * features.shape[0] * length * plane_count * length
    local_sum = product("sczyx,szyx->c", features_wide, vol_grad) / voxel_count
    w_grad = lax.psum(local_sum, ("dp", "slab"))
    return (vol_grad, w_grad)


def fourier_tables(length):
    half, quarter = length // 2, length // 4
    index = np.arange(length)
    angle = (index[:, None] * index[None, :] % length) * (2.0 * np.pi / length)
    cos, sin = np.cos(angle), np.sin(angle)
    columns = []
    for first in (0, quarter):
        columns += [cos[:, first:first + quarter], -sin[:, first:first + quarter]]
    along = np.concatenate(columns, axis=1)
    along[:, quarter] = cos[:, half]
    parts = []
    for table in (along, cos, sin, along.T):
        high = table.astype(jnp.bfloat16)
        parts += [high, (table - high.astype(np.float64)).astype(jnp.bfloat16)]
    return np.stack(parts)


def halves(value):
    high = value.astype(jnp.bfloat16)
    return high, (value - high.astype(jnp.float32)).astype(jnp.bfloat16)


def dot(left, right):
    return jnp.dot(left, right, preferred_element_type=jnp.float32)


def dot3(left, right):
    return dot(left[0], right[0]) + (dot(left[0], right[1]) + dot(left[1], right[0]))


def kernel(
    dp_count, slab_count, voxel_count,
    rotation, weight_hbm, blocks_hbm, features_hbm, target_hbm, wedge_hbm, tables_hbm,
    out, out_sums,
    weight, blocks, features, target, wedge, tables, outgoing, plane, direct, cross, back, returned,
    sums, own_sum, all_sums,
    load_sem, side_sem, send_sem, recv_sem, send2_sem, recv2_sem, sum_send_sem, sum_recv_sem,
):
    channels, depth, planes, length = features.shape
    pieces = depth // ROWS
    half, quarter = length // 2, length // 4
    my_dp, me = lax.axis_index("dp"), lax.axis_index("slab")
    slab_steps = range(slab_count - 1, 0, -1)

    def slab_peer(step):
        return lax.bitwise_xor(me, jnp.int32(step))

    def dp_peer(step):
        return lax.rem(my_dp + step, dp_count)

    loads = []
    for j in range(pieces):
        rows = pl.ds(j * ROWS, ROWS)
        loads.append(pltpu.make_async_copy(features_hbm.at[:, rows], features.at[:, rows], load_sem.at[j]))
    sides = [
        pltpu.make_async_copy(weight_hbm, weight, side_sem.at[0]),
        pltpu.make_async_copy(target_hbm, target, side_sem.at[1]),
        pltpu.make_async_copy(tables_hbm.at[0:2], tables.at[0:2], side_sem.at[2]),
        pltpu.make_async_copy(blocks_hbm, blocks, side_sem.at[3]),
        pltpu.make_async_copy(wedge_hbm, wedge, side_sem.at[4]),
        pltpu.make_async_copy(tables_hbm.at[2:8], tables.at[2:8], side_sem.at[5]),
    ]
    barrier = pltpu.get_barrier_semaphore()
    for r in slab_steps:
        pl.semaphore_signal(barrier, inc=1, device_id=(my_dp, slab_peer(r)), device_id_type=MESH)
    for r in range(1, dp_count):
        pl.semaphore_signal(barrier, inc=1, device_id=(dp_peer(r), me), device_id_type=MESH)
    for copy in (*sides[:2], loads[0], sides[2], *loads[1:], *sides[3:]):
        copy.start()

    def table(k):
        return tables[2 * k], tables[2 * k + 1]

    arrivals, departures = {}, []

    def exchange(kind, h, first, count, source, landing, sends, recvs):
        group = len([key for key in arrivals if key[0] == kind])
        arrivals[kind, h, first] = []
        for r in slab_steps:
            peer = slab_peer(r)
            copy = pltpu.make_async_remote_copy(
                src_ref=source.at[h, peer, pl.ds(first * ROWS, count * ROWS)],
                dst_ref=landing.at[h, me, pl.ds(first * ROWS, count * ROWS)],
                send_sem=sends.at[r - 1, group],
                recv_sem=recvs.at[r - 1, group],
                device_id=(my_dp, peer),
                device_id_type=MESH,
            )
            copy.start()
            arrivals[kind, h, first].append(copy)
            departures.append(copy)

    for j in range(pieces):
        base = j * ROWS
        if j == 0:
            sides[0].wait()
            sides[1].wait()
        loads[j].wait()

        def add_channel(c, accs):
            scale = weight[c]
            return tuple(
                accs[z] + scale * features[c, base + z].astype(jnp.float32) for z in range(ROWS)
            )

        start = tuple(-target[base + z].astype(jnp.float32) for z in range(ROWS))
        accs = lax.fori_loop(0, channels, add_channel, start, unroll=4)
        if j == 0:
            sides[2].wait()
        lines = dot3(halves(jnp.concatenate(accs, axis=0)), table(0))
        lines = jnp.swapaxes(lines.reshape(ROWS, planes, length), 0, 1)
        for h in range(2):
            outgoing[h, :, pl.ds(base, ROWS), :] = lines[:, :, h * half:(h + 1) * half]
            plane[h, me, pl.ds(base, ROWS), :] = outgoing[h, me, pl.ds(base, ROWS), :]
        if j == 0:
            pl.semaphore_wait(barrier, slab_count + dp_count - 2)
        exchange("out", 0, j, 1, outgoing, plane, send_sem, recv_sem)
    for first in range(0, pieces, OUT_GROUP):
        exchange("out", 1, first, OUT_GROUP, outgoing, plane, send_sem, recv_sem)

    sides[3].wait()
    sides[4].wait()
    row = lax.broadcasted_iota(jnp.int32, (length, length), 0)
    column = lax.broadcasted_iota(jnp.int32, (length, length), 1)
    row_block, column_block = row // BLK, column // BLK
    listed = jnp.zeros((length, length), jnp.bool_)
    for n in range(blocks.shape[1]):
        listed = listed | ((row_block == blocks[0, n]) & (column_block == blocks[1, n]))
    mask = jnp.where(listed, wedge[...], 0).astype(jnp.float32)
    mirror = jnp.where(lax.rem(row + column, length) == 0, 1.0, 0.0).astype(jnp.bfloat16)
    flipped = dot(dot(mirror, mask.astype(jnp.bfloat16)).astype(jnp.bfloat16), mirror)
    even = mask + flipped
    odd = lax.dot_general(
        even.astype(jnp.bfloat16), mirror, (((0,), (0,)), ((), ())), preferred_element_type=jnp.float32
    )
    is_odd = lax.rem(rotation[0], 2) == 1
    kept = jnp.where(is_odd, odd, even).astype(jnp.bfloat16)
    within = lax.rem(column, half)
    alone = lax.rem(column, quarter) + column // half == 0
    lane_freq = jnp.where(column == quarter, half, lax.rem(within, quarter) + column // half * quarter)
    spread = dot(kept, jnp.where(row == lane_freq, 1.0, 0.0).astype(jnp.bfloat16))
    scale = 1.0 / (length * length)
    direct[...] = spread * jnp.where(alone, scale, 2.0 * scale)
    cross[...] = spread * jnp.where(alone, 0.0, jnp.where(within < quarter, 2.0 * scale, -2.0 * scale))
    sides[5].wait()

    for h in range(2):
        for key in [key for key in arrivals if key[:2] == ("out", h)]:
            for copy in arrivals[key]:
                copy.wait_recv()
        lines = halves(plane[h].reshape(length, half))
        even_part, odd_part = dot3(table(1), lines), dot3(table(2), lines)
        own, other = direct[:, h * half:(h + 1) * half], cross[:, h * half:(h + 1) * half]
        first = halves(own * even_part + other * pltpu.roll(odd_part, quarter, 1))
        second = halves(own * odd_part - other * pltpu.roll(even_part, quarter, 1))
        back[h] = (dot3(table(1), first) + dot3(table(2), second)).reshape(slab_count, depth, half)
        step = BACK_GROUPS[h]
        for j in range(0, pieces, step):
            exchange("back", h, j, step, back, returned, send2_sem, recv2_sem)
        returned[h, me] = back[h, me]

    for j in range(pieces):
        base = j * ROWS
        for h in range(2):
            for copy in arrivals.get(("back", h, j), []):
                copy.wait_recv()
        lines = jnp.concatenate(
            [returned[h, :, pl.ds(base, ROWS), :].reshape(planes * ROWS, half) for h in range(2)], axis=1
        )
        piece = dot3(halves(lines), table(3)).reshape(planes, ROWS, length)
        piece = jnp.swapaxes(piece, 0, 1)
        out[pl.ds(base, ROWS)] = piece
        grads = [piece[z] for z in range(ROWS)]

        def channel_sum(c, carry):
            acc = grads[0] * features[c, base].astype(jnp.float32)
            for z in range(1, ROWS):
                acc = acc + grads[z] * features[c, base + z].astype(jnp.float32)
            folded = acc[:, :128]
            for lane in range(128, length, 128):
                folded = folded + acc[:, lane:lane + 128]
            sums[c] = folded if j == 0 else sums[c] + folded
            return carry

        lax.fori_loop(0, channels, channel_sum, 0, unroll=4)

    rest = jnp.sum(sums[...], axis=1)
    ones = jnp.ones((8, 128), jnp.bfloat16)
    row_sum = jnp.zeros((8, channels), jnp.float32)
    for _ in range(3):
        part = rest.astype(jnp.bfloat16)
        rest = rest - part.astype(jnp.float32)
        row_sum = row_sum + lax.dot_general(
            ones, part, (((1,), (1,)), ((), ())), preferred_element_type=jnp.float32
        )
    row_sum = row_sum[0:1]
    own_sum[0] = row_sum
    place = my_dp * slab_count + me
    totals = []
    for r in range(slab_count - 1, -1, -1):
        for k in range(dp_count - 1, -1, -1):
            if k == 0 and r == 0:
                continue
            copy = pltpu.make_async_remote_copy(
                src_ref=own_sum.at[0],
                dst_ref=all_sums.at[place],
                send_sem=sum_send_sem.at[k, r],
                recv_sem=sum_recv_sem.at[k, r],
                device_id=(dp_peer(k), slab_peer(r)),
                device_id_type=MESH,
            )
            copy.start()
            totals.append(copy)
    all_sums[place] = row_sum
    for copy in departures:
        copy.wait_send()
    for copy in totals:
        copy.wait()
    out_sums[...] = jnp.sum(all_sums[...], axis=0) / voxel_count


def hand_over(vol_grad, w_grad, out, out_weight_grad, sem):
    copies = [
        pltpu.make_async_copy(vol_grad, out, sem.at[0]),
        pltpu.make_async_copy(w_grad, out_weight_grad, sem.at[1]),
    ]
    for copy in copies:
        copy.start()
    for copy in copies:
        copy.wait()


def split_planes(features, target, out_weight, rotation, blocks, wedge):
    _, channels, depth, planes, length = features.shape
    dp_count, slab_count = lax.axis_size("dp"), lax.axis_size("slab")
    pieces = depth // ROWS
    half = length // 2
    voxel_count = dp_count * length * planes * length
    smem = pl.BlockSpec(memory_space=pltpu.SMEM)
    hbm = pl.BlockSpec(memory_space=pltpu.HBM)
    vmem = pl.BlockSpec(memory_space=pltpu.VMEM)
    dma = pltpu.SemaphoreType.DMA
    out_groups = pieces + pieces // OUT_GROUP
    back_groups = pieces // BACK_GROUPS[0] + pieces // BACK_GROUPS[1]
    vol_grad, w_grad = pl.pallas_call(
        functools.partial(kernel, dp_count, slab_count, float(voxel_count)),
        out_shape=(
            pltpu.VMEM((depth, planes, length), jnp.float32),
            pltpu.VMEM((1, channels), jnp.float32),
        ),
        in_specs=[smem, hbm, hbm, hbm, hbm, hbm, hbm],
        out_specs=(vmem, vmem),
        scratch_shapes=[
            pltpu.SMEM((channels,), jnp.float32),
            pltpu.SMEM((2, blocks.shape[0]), jnp.int32),
            pltpu.VMEM((channels, depth, planes, length), jnp.bfloat16),
            pltpu.VMEM((depth, planes, length), jnp.bfloat16),
            pltpu.VMEM((length, length), jnp.int32),
            pltpu.VMEM((8, length, length), jnp.bfloat16),
            pltpu.VMEM((2, planes, depth, half), jnp.float32),
            pltpu.VMEM((2, slab_count, depth, half), jnp.float32),
            pltpu.VMEM((length, length), jnp.float32),
            pltpu.VMEM((length, length), jnp.float32),
            pltpu.VMEM((2, slab_count, depth, half), jnp.float32),
            pltpu.VMEM((2, planes, depth, half), jnp.float32),
            pltpu.VMEM((channels, 8, 128), jnp.float32),
            pltpu.VMEM((1, 1, channels), jnp.float32),
            pltpu.VMEM((dp_count * slab_count, 1, channels), jnp.float32),
            dma((pieces,)),
            dma((6,)),
            dma((slab_count - 1, out_groups)),
            dma((slab_count - 1, out_groups)),
            dma((slab_count - 1, back_groups)),
            dma((slab_count - 1, back_groups)),
            dma((dp_count, slab_count)),
            dma((dp_count, slab_count)),
        ],
        compiler_params=pltpu.CompilerParams(
            collective_id=0, has_side_effects=True, vmem_limit_bytes=56 * 1024 * 1024
        ),
    )(
        rotation, out_weight, blocks.T, features[0], target[0], wedge, jnp.asarray(fourier_tables(length)),
    )
    vol_grad, w_grad = pl.pallas_call(
        hand_over,
        out_shape=(
            jax.ShapeDtypeStruct(vol_grad.shape, jnp.float32),
            jax.ShapeDtypeStruct(w_grad.shape, jnp.float32),
        ),
        in_specs=[vmem, vmem],
        out_specs=(hbm, hbm),
        scratch_shapes=[dma((2,))],
    )(
        pltpu.with_memory_space_constraint(vol_grad, pltpu.VMEM),
        pltpu.with_memory_space_constraint(w_grad, pltpu.VMEM),
    )
    return vol_grad[None], w_grad[0]


def solution(mesh):
    def on_device(features, *rest):
        samples, _, depth, planes, length = features.shape
        whole_planes = (
            samples == 1
            and planes == 8
            and planes == mesh.shape["slab"]
            and depth % (4 * ROWS) == 0
            and length % 256 == 0
        )
        return (split_planes if whole_planes else split_lines)(features, *rest)

    in_specs = (
        P("dp", None, "slab", None, None),
        P("dp", "slab", None, None),
        P(),
        P("dp"),
        P(),
        P(),
    )
    out_specs = (P("dp", "slab", None, None), P())
    return jax.shard_map(
        on_device, mesh=mesh, in_specs=in_specs, out_specs=out_specs, check_vma=False
    )
```

```python
import functools
import math

import numpy as np

import jax
import jax.numpy as jnp
from jax import lax
from jax.experimental import pallas as pl
from jax.experimental.pallas import tpu as pltpu
from jax.sharding import PartitionSpec as P

BLK = 64
ROWS = 8
OUT_GROUP = 4
HELD = 2
AT_ONCE = 8
SUMMED = 16
SPREAD = (5, 2, 1)
BACK_GROUPS = (4, 1)
MESH = pl.DeviceIdType.MESH


def product(form, left, right):
    return jnp.einsum(form, left, right, precision=lax.Precision.HIGHEST)


def wedge_weights(blocks, wedge, length):
    per_side = length // BLK
    labels = jnp.arange(per_side, dtype=jnp.int32)
    match = (blocks[:, 0][:, None, None] == labels[None, :, None]) & (
        blocks[:, 1][:, None, None] == labels[None, None, :]
    )
    listed = jnp.any(match, axis=0)
    spread = jnp.repeat(jnp.repeat(listed, BLK, axis=0), BLK, axis=1)
    return jnp.where(spread, wedge, 0).astype(jnp.float32)


def phase_tables(turns, length):
    positions = jnp.arange(length, dtype=jnp.int32)
    flip_depth = turns >= 2
    flip_width = (turns == 1) | (turns == 2)
    depth_index = jnp.where(
        flip_depth[:, None], length - 1 - positions[None, :], positions[None, :]
    )
    width_index = jnp.where(
        flip_width[:, None], length - 1 - positions[None, :], positions[None, :]
    )
    depth_phase = positions[None, :, None] * depth_index[:, None, :] % length
    width_phase = width_index[:, :, None] * positions[None, None, :] % length
    depth_angle = depth_phase.astype(jnp.float32) * (2.0 * math.pi / length)
    width_angle = width_phase.astype(jnp.float32) * (2.0 * math.pi / length)
    return (jnp.cos(depth_angle), jnp.sin(depth_angle), jnp.cos(width_angle), jnp.sin(width_angle))


def split_lines(features, target, out_weight, rotation, blocks, wedge):
    length = features.shape[-1]
    plane_count = features.shape[3]
    slab_count = lax.axis_size("slab")
    columns = length // slab_count
    col_start = lax.axis_index("slab") * columns
    features_wide = features.astype(jnp.float32)
    volume = product("c,sczyx->szyx", out_weight, features_wide)
    difference = volume - target.astype(jnp.float32)
    depth_cos, depth_sin, width_cos, width_sin = phase_tables(rotation, length)
    line_real = product("szyb,sbp->szyp", difference, width_cos)
    line_imag = -product("szyb,sbp->szyp", difference, width_sin)
    line_real, line_imag = (
        lax.all_to_all(line_real, "slab", split_axis=3, concat_axis=1, tiled=True),
        lax.all_to_all(line_imag, "slab", split_axis=3, concat_axis=1, tiled=True),
    )
    spec_real = (
        product("spa,sayq->spyq", depth_cos, line_real)
        + product("spa,sayq->spyq", depth_sin, line_imag)
    ) / length
    spec_imag = (
        product("spa,sayq->spyq", depth_cos, line_imag)
        - product("spa,sayq->spyq", depth_sin, line_real)
    ) / length
    mask = wedge_weights(blocks, wedge, length)
    odd_turn = rotation % 2 == 1
    mask_turned = jnp.where(odd_turn[:, None, None], mask.T[None], mask[None])
    mask_columns = lax.dynamic_slice_in_dim(mask_turned, col_start, columns, 2)
    grad_real = 2.0 * mask_columns[:, :, None, :] * spec_real
    grad_imag = 2.0 * mask_columns[:, :, None, :] * spec_imag
    back_real = product("spa,spyq->sayq", depth_cos, grad_real) - product(
        "spa,spyq->sayq", depth_sin, grad_imag
    )
    back_imag = product("spa,spyq->sayq", depth_cos, grad_imag) + product(
        "spa,spyq->sayq", depth_sin, grad_real
    )
    back_real, back_imag = (
        lax.all_to_all(back_real, "slab", split_axis=1, concat_axis=3, tiled=True),
        lax.all_to_all(back_imag, "slab", split_axis=1, concat_axis=3, tiled=True),
    )
    vol_grad = (
        product("sayp,sbp->sayb", back_real, width_cos)
        - product("sayp,sbp->sayb", back_imag, width_sin)
    ) / length
    voxel_count = lax.axis_size("dp") * features.shape[0] * length * plane_count * length
    local_sum = product("sczyx,szyx->c", features_wide, vol_grad) / voxel_count
    w_grad = lax.psum(local_sum, ("dp", "slab"))
    return (vol_grad, w_grad)


def fourier_tables(length):
    half, quarter = length // 2, length // 4
    index = np.arange(length)
    angle = (index[:, None] * index[None, :] % length) * (2.0 * np.pi / length)
    cos, sin = np.cos(angle), np.sin(angle)
    columns = []
    for first in (0, quarter):
        columns += [cos[:, first:first + quarter], -sin[:, first:first + quarter]]
    along = np.concatenate(columns, axis=1)
    along[:, quarter] = cos[:, half]
    parts = []
    for table in (along, cos, sin, along.T):
        high = table.astype(jnp.bfloat16)
        parts += [high, (table - high.astype(np.float64)).astype(jnp.bfloat16)]
    return np.stack(parts)


def halves(value):
    high = value.astype(jnp.bfloat16)
    return high, (value - high.astype(jnp.float32)).astype(jnp.bfloat16)


def dot(left, right):
    return jnp.dot(left, right, preferred_element_type=jnp.float32)


def dot3(left, right):
    return dot(left[0], right[0]) + (dot(left[0], right[1]) + dot(left[1], right[0]))


def kernel(
    dp_count, slab_count, voxel_count,
    rotation, weight_hbm, blocks_hbm, features_hbm, target_hbm, wedge_hbm, tables_hbm,
    out, out_sums,
    weight, blocks, features, target, wedge, tables, outgoing, plane, direct, cross, back, returned,
    spread_features, turned, sums, own_sum, all_sums,
    load_sem, side_sem, send_sem, recv_sem, send2_sem, recv2_sem, sum_send_sem, sum_recv_sem,
):
    channels, depth, planes, length = features.shape
    pieces = depth // ROWS
    half, quarter = length // 2, length // 4
    my_dp, me = lax.axis_index("dp"), lax.axis_index("slab")
    slab_steps = range(slab_count - 1, 0, -1)

    def slab_peer(step):
        return lax.bitwise_xor(me, jnp.int32(step))

    def dp_peer(step):
        return lax.rem(my_dp + step, dp_count)

    loads = []
    for j in range(pieces):
        rows = pl.ds(j * ROWS, ROWS)
        loads.append(pltpu.make_async_copy(features_hbm.at[:, rows], features.at[:, rows], load_sem.at[j]))
    sides = [
        pltpu.make_async_copy(weight_hbm, weight, side_sem.at[0]),
        pltpu.make_async_copy(target_hbm, target, side_sem.at[1]),
        pltpu.make_async_copy(tables_hbm.at[0:2], tables.at[0:2], side_sem.at[2]),
        pltpu.make_async_copy(blocks_hbm, blocks, side_sem.at[3]),
        pltpu.make_async_copy(wedge_hbm, wedge, side_sem.at[4]),
        pltpu.make_async_copy(tables_hbm.at[2:8], tables.at[2:8], side_sem.at[5]),
    ]
    barrier = pltpu.get_barrier_semaphore()
    for r in slab_steps:
        pl.semaphore_signal(barrier, inc=1, device_id=(my_dp, slab_peer(r)), device_id_type=MESH)
    for r in range(1, dp_count):
        pl.semaphore_signal(barrier, inc=1, device_id=(dp_peer(r), me), device_id_type=MESH)
    for copy in (*sides[:2], loads[0], sides[2], *loads[1:], *sides[3:]):
        copy.start()

    def table(k):
        return tables[2 * k], tables[2 * k + 1]

    arrivals, departures = {}, []

    def all_but_one(ref, sem, *index):
        part = ref.at[index[0], pl.ds(0, slab_count - 1), index[1]]
        return pltpu.make_async_copy(part, part, sem)

    def exchange(kind, h, first, count, source, landing, sends, recvs):
        group = len([key for key in arrivals if key[0] == kind])
        rows = pl.ds(first * ROWS, count * ROWS)
        for r in slab_steps:
            peer = slab_peer(r)
            pltpu.make_async_remote_copy(
                src_ref=source.at[h, peer, rows],
                dst_ref=landing.at[h, me, rows],
                send_sem=sends.at[group],
                recv_sem=recvs.at[group],
                device_id=(my_dp, peer),
                device_id_type=MESH,
            ).start()
        arrivals[kind, h, first] = all_but_one(landing, recvs.at[group], h, rows)
        departures.append(all_but_one(source, sends.at[group], h, rows))

    for j in range(pieces):
        base = j * ROWS
        if j == 0:
            sides[0].wait()
            sides[1].wait()
        loads[j].wait()

        def add_channel(c, accs):
            scale = weight[c]
            return tuple(
                accs[z] + scale * features[c, base + z].astype(jnp.float32) for z in range(ROWS)
            )

        start = tuple(-target[base + z].astype(jnp.float32) for z in range(ROWS))
        accs = lax.fori_loop(0, channels, add_channel, start, unroll=4)
        if j == 0:
            sides[2].wait()
        lines = dot3(halves(jnp.concatenate(accs, axis=0)), table(0))
        lines = jnp.swapaxes(lines.reshape(ROWS, planes, length), 0, 1)
        for h in range(2):
            outgoing[h, :, pl.ds(base, ROWS), :] = lines[:, :, h * half:(h + 1) * half]
            plane[h, me, pl.ds(base, ROWS), :] = outgoing[h, me, pl.ds(base, ROWS), :]
        if j < HELD - 1:
            continue
        first = j
        if j == HELD - 1:
            pl.semaphore_wait(barrier, slab_count + dp_count - 2)
            first = 0
        exchange("out", 0, first, j + 1 - first, outgoing, plane, send_sem, recv_sem)
    for first in range(0, pieces, OUT_GROUP):
        exchange("out", 1, first, OUT_GROUP, outgoing, plane, send_sem, recv_sem)

    def transform_channels(first, groups):
        def transform(i, carry):
            for u in range(AT_ONCE):
                c = (first + i) * AT_ONCE + u
                rows = features[c].reshape(depth * planes, length)
                lines = dot(rows, tables[0]) + dot(rows, tables[1])
                for h in range(2):
                    spread_features[h, c] = lines[:, h * half:(h + 1) * half].reshape(depth, planes, half)
            return carry

        lax.fori_loop(0, groups, transform, 0)

    sides[3].wait()
    sides[4].wait()
    row = lax.broadcasted_iota(jnp.int32, (length, length), 0)
    column = lax.broadcasted_iota(jnp.int32, (length, length), 1)
    row_block, column_block = row // BLK, column // BLK
    listed = jnp.zeros((length, length), jnp.bool_)
    for n in range(blocks.shape[1]):
        listed = listed | ((row_block == blocks[0, n]) & (column_block == blocks[1, n]))
    mask = jnp.where(listed, wedge[...], 0).astype(jnp.float32)
    mirror = jnp.where(lax.rem(row + column, length) == 0, 1.0, 0.0).astype(jnp.bfloat16)
    flipped = dot(dot(mirror, mask.astype(jnp.bfloat16)).astype(jnp.bfloat16), mirror)
    even = mask + flipped
    odd = lax.dot_general(
        even.astype(jnp.bfloat16), mirror, (((0,), (0,)), ((), ())), preferred_element_type=jnp.float32
    )
    is_odd = lax.rem(rotation[0], 2) == 1
    kept = jnp.where(is_odd, odd, even).astype(jnp.bfloat16)
    within = lax.rem(column, half)
    alone = lax.rem(column, quarter) + column // half == 0
    lane_freq = jnp.where(column == quarter, half, lax.rem(within, quarter) + column // half * quarter)
    spread = dot(kept, jnp.where(row == lane_freq, 1.0, 0.0).astype(jnp.bfloat16))
    scale = 1.0 / (length * length)
    direct[...] = spread * jnp.where(alone, scale, 2.0 * scale)
    cross[...] = spread * jnp.where(alone, 0.0, jnp.where(within < quarter, 2.0 * scale, -2.0 * scale))
    sides[5].wait()
    transform_channels(0, SPREAD[0])

    for h in range(2):
        for key in [key for key in arrivals if key[:2] == ("out", h)]:
            arrivals[key].wait()
        lines = halves(plane[h].reshape(length, half))
        even_part, odd_part = dot3(table(1), lines), dot3(table(2), lines)
        own, other = direct[:, h * half:(h + 1) * half], cross[:, h * half:(h + 1) * half]
        first = halves(own * even_part + other * pltpu.roll(odd_part, quarter, 1))
        second = halves(own * odd_part - other * pltpu.roll(even_part, quarter, 1))
        back[h] = (dot3(table(1), first) + dot3(table(2), second)).reshape(slab_count, depth, half)
        step = BACK_GROUPS[h]
        for j in range(0, pieces, step):
            exchange("back", h, j, step, back, returned, send2_sem, recv2_sem)
        returned[h, me] = back[h, me]
        transform_channels(sum(SPREAD[:h + 1]), SPREAD[h + 1])

    for h in range(2):
        for j in range(pieces):
            base = j * ROWS
            if ("back", h, j) in arrivals:
                arrivals["back", h, j].wait()
            lines = jnp.swapaxes(returned[h, :, pl.ds(base, ROWS), :], 0, 1)
            turned[h, pl.ds(base, ROWS)] = lines

            def channel_sums(i, carry):
                first = i * SUMMED
                accs = [lines[0] * spread_features[h, first + u, base] for u in range(SUMMED)]
                for z in range(1, ROWS):
                    accs = [accs[u] + lines[z] * spread_features[h, first + u, base + z] for u in range(SUMMED)]
                for u in range(SUMMED):
                    sums[first + u] = accs[u] if h + j == 0 else sums[first + u] + accs[u]
                return carry

            lax.fori_loop(0, channels // SUMMED, channel_sums, 0)

    rest = jnp.sum(sums[...], axis=1)
    ones = jnp.ones((8, 128), jnp.bfloat16)
    row_sum = jnp.zeros((8, channels), jnp.float32)
    for _ in range(3):
        part = rest.astype(jnp.bfloat16)
        rest = rest - part.astype(jnp.float32)
        row_sum = row_sum + lax.dot_general(
            ones, part, (((1,), (1,)), ((), ())), preferred_element_type=jnp.float32
        )
    row_sum = row_sum[0:1]
    own_sum[0] = row_sum
    place = my_dp * slab_count + me
    for r in range(slab_count - 1, -1, -1):
        for k in range(dp_count - 1, -1, -1):
            if k == 0 and r == 0:
                continue
            pltpu.make_async_remote_copy(
                src_ref=own_sum.at[0],
                dst_ref=all_sums.at[place],
                send_sem=sum_send_sem.at[0],
                recv_sem=sum_recv_sem.at[0],
                device_id=(dp_peer(k), slab_peer(r)),
                device_id_type=MESH,
            ).start()
    all_sums[place] = row_sum
    lines = jnp.concatenate([turned[h].reshape(depth * planes, half) for h in range(2)], axis=1)
    out[...] = dot3(halves(lines), table(3)).reshape(depth, planes, length)
    for copy in departures:
        copy.wait()
    others = all_sums.at[pl.ds(0, dp_count * slab_count - 1)]
    pltpu.make_async_copy(others, others, sum_recv_sem.at[0]).wait()
    pltpu.make_async_copy(others, others, sum_send_sem.at[0]).wait()
    out_sums[...] = jnp.sum(all_sums[...], axis=0) / voxel_count


def hand_over(vol_grad, w_grad, out, out_weight_grad, sem):
    copies = [
        pltpu.make_async_copy(vol_grad, out, sem.at[0]),
        pltpu.make_async_copy(w_grad, out_weight_grad, sem.at[1]),
    ]
    for copy in copies:
        copy.start()
    for copy in copies:
        copy.wait()


def split_planes(features, target, out_weight, rotation, blocks, wedge):
    _, channels, depth, planes, length = features.shape
    dp_count, slab_count = lax.axis_size("dp"), lax.axis_size("slab")
    pieces = depth // ROWS
    half = length // 2
    voxel_count = dp_count * length * planes * length
    smem = pl.BlockSpec(memory_space=pltpu.SMEM)
    hbm = pl.BlockSpec(memory_space=pltpu.HBM)
    vmem = pl.BlockSpec(memory_space=pltpu.VMEM)
    dma = pltpu.SemaphoreType.DMA
    out_groups = pieces - HELD + 1 + pieces // OUT_GROUP
    back_groups = pieces // BACK_GROUPS[0] + pieces // BACK_GROUPS[1]
    vol_grad, w_grad = pl.pallas_call(
        functools.partial(kernel, dp_count, slab_count, float(voxel_count)),
        out_shape=(
            pltpu.VMEM((depth, planes, length), jnp.float32),
            pltpu.VMEM((1, channels), jnp.float32),
        ),
        in_specs=[smem, hbm, hbm, hbm, hbm, hbm, hbm],
        out_specs=(vmem, vmem),
        scratch_shapes=[
            pltpu.SMEM((channels,), jnp.float32),
            pltpu.SMEM((2, blocks.shape[0]), jnp.int32),
            pltpu.VMEM((channels, depth, planes, length), jnp.bfloat16),
            pltpu.VMEM((depth, planes, length), jnp.bfloat16),
            pltpu.VMEM((length, length), jnp.int32),
            pltpu.VMEM((8, length, length), jnp.bfloat16),
            pltpu.VMEM((2, planes, depth, half), jnp.float32),
            pltpu.VMEM((2, slab_count, depth, half), jnp.float32),
            pltpu.VMEM((length, length), jnp.float32),
            pltpu.VMEM((length, length), jnp.float32),
            pltpu.VMEM((2, slab_count, depth, half), jnp.float32),
            pltpu.VMEM((2, planes, depth, half), jnp.float32),
            pltpu.VMEM((2, channels, depth, planes, half), jnp.float32),
            pltpu.VMEM((2, depth, planes, half), jnp.float32),
            pltpu.VMEM((channels, planes, half), jnp.float32),
            pltpu.VMEM((1, 1, channels), jnp.float32),
            pltpu.VMEM((dp_count * slab_count, 1, channels), jnp.float32),
            dma((pieces,)),
            dma((6,)),
            dma((out_groups,)),
            dma((out_groups,)),
            dma((back_groups,)),
            dma((back_groups,)),
            dma((1,)),
            dma((1,)),
        ],
        compiler_params=pltpu.CompilerParams(
            collective_id=0, has_side_effects=True, vmem_limit_bytes=56 * 1024 * 1024
        ),
    )(
        rotation, out_weight, blocks.T, features[0], target[0], wedge, jnp.asarray(fourier_tables(length)),
    )
    vol_grad, w_grad = pl.pallas_call(
        hand_over,
        out_shape=(
            jax.ShapeDtypeStruct(vol_grad.shape, jnp.float32),
            jax.ShapeDtypeStruct(w_grad.shape, jnp.float32),
        ),
        in_specs=[vmem, vmem],
        out_specs=(hbm, hbm),
        scratch_shapes=[dma((2,))],
    )(
        pltpu.with_memory_space_constraint(vol_grad, pltpu.VMEM),
        pltpu.with_memory_space_constraint(w_grad, pltpu.VMEM),
    )
    return vol_grad[None], w_grad[0]


def solution(mesh):
    def on_device(features, *rest):
        samples, _, depth, planes, length = features.shape
        whole_planes = (
            samples == 1
            and planes == 8
            and planes == mesh.shape["slab"]
            and depth % (4 * ROWS) == 0
            and length % 256 == 0
            and features.shape[1] % (AT_ONCE * sum(SPREAD)) == 0
        )
        return (split_planes if whole_planes else split_lines)(features, *rest)

    in_specs = (
        P("dp", None, "slab", None, None),
        P("dp", "slab", None, None),
        P(),
        P("dp"),
        P(),
        P(),
    )
    out_specs = (P("dp", "slab", None, None), P())
    return jax.shard_map(
        on_device, mesh=mesh, in_specs=in_specs, out_specs=out_specs, check_vma=False
    )
```

```python
import functools
import math

import numpy as np

import jax
import jax.numpy as jnp
from jax import lax
from jax.experimental import pallas as pl
from jax.experimental.pallas import tpu as pltpu
from jax.sharding import PartitionSpec as P

BLK = 64
ROWS = 8
OUT_GROUP = 2
HELD = 2
AT_ONCE = 8
SUMMED = 16
SPREAD = (4, 2, 2)
BACK_GROUPS = (4, 1)
MESH = pl.DeviceIdType.MESH


def product(form, left, right):
    return jnp.einsum(form, left, right, precision=lax.Precision.HIGHEST)


def wedge_weights(blocks, wedge, length):
    per_side = length // BLK
    labels = jnp.arange(per_side, dtype=jnp.int32)
    match = (blocks[:, 0][:, None, None] == labels[None, :, None]) & (
        blocks[:, 1][:, None, None] == labels[None, None, :]
    )
    listed = jnp.any(match, axis=0)
    spread = jnp.repeat(jnp.repeat(listed, BLK, axis=0), BLK, axis=1)
    return jnp.where(spread, wedge, 0).astype(jnp.float32)


def phase_tables(turns, length):
    positions = jnp.arange(length, dtype=jnp.int32)
    flip_depth = turns >= 2
    flip_width = (turns == 1) | (turns == 2)
    depth_index = jnp.where(
        flip_depth[:, None], length - 1 - positions[None, :], positions[None, :]
    )
    width_index = jnp.where(
        flip_width[:, None], length - 1 - positions[None, :], positions[None, :]
    )
    depth_phase = positions[None, :, None] * depth_index[:, None, :] % length
    width_phase = width_index[:, :, None] * positions[None, None, :] % length
    depth_angle = depth_phase.astype(jnp.float32) * (2.0 * math.pi / length)
    width_angle = width_phase.astype(jnp.float32) * (2.0 * math.pi / length)
    return (jnp.cos(depth_angle), jnp.sin(depth_angle), jnp.cos(width_angle), jnp.sin(width_angle))


def split_lines(features, target, out_weight, rotation, blocks, wedge):
    length = features.shape[-1]
    plane_count = features.shape[3]
    slab_count = lax.axis_size("slab")
    columns = length // slab_count
    col_start = lax.axis_index("slab") * columns
    features_wide = features.astype(jnp.float32)
    volume = product("c,sczyx->szyx", out_weight, features_wide)
    difference = volume - target.astype(jnp.float32)
    depth_cos, depth_sin, width_cos, width_sin = phase_tables(rotation, length)
    line_real = product("szyb,sbp->szyp", difference, width_cos)
    line_imag = -product("szyb,sbp->szyp", difference, width_sin)
    line_real, line_imag = (
        lax.all_to_all(line_real, "slab", split_axis=3, concat_axis=1, tiled=True),
        lax.all_to_all(line_imag, "slab", split_axis=3, concat_axis=1, tiled=True),
    )
    spec_real = (
        product("spa,sayq->spyq", depth_cos, line_real)
        + product("spa,sayq->spyq", depth_sin, line_imag)
    ) / length
    spec_imag = (
        product("spa,sayq->spyq", depth_cos, line_imag)
        - product("spa,sayq->spyq", depth_sin, line_real)
    ) / length
    mask = wedge_weights(blocks, wedge, length)
    odd_turn = rotation % 2 == 1
    mask_turned = jnp.where(odd_turn[:, None, None], mask.T[None], mask[None])
    mask_columns = lax.dynamic_slice_in_dim(mask_turned, col_start, columns, 2)
    grad_real = 2.0 * mask_columns[:, :, None, :] * spec_real
    grad_imag = 2.0 * mask_columns[:, :, None, :] * spec_imag
    back_real = product("spa,spyq->sayq", depth_cos, grad_real) - product(
        "spa,spyq->sayq", depth_sin, grad_imag
    )
    back_imag = product("spa,spyq->sayq", depth_cos, grad_imag) + product(
        "spa,spyq->sayq", depth_sin, grad_real
    )
    back_real, back_imag = (
        lax.all_to_all(back_real, "slab", split_axis=1, concat_axis=3, tiled=True),
        lax.all_to_all(back_imag, "slab", split_axis=1, concat_axis=3, tiled=True),
    )
    vol_grad = (
        product("sayp,sbp->sayb", back_real, width_cos)
        - product("sayp,sbp->sayb", back_imag, width_sin)
    ) / length
    voxel_count = lax.axis_size("dp") * features.shape[0] * length * plane_count * length
    local_sum = product("sczyx,szyx->c", features_wide, vol_grad) / voxel_count
    w_grad = lax.psum(local_sum, ("dp", "slab"))
    return (vol_grad, w_grad)


def fourier_tables(length):
    half, quarter = length // 2, length // 4
    index = np.arange(length)
    angle = (index[:, None] * index[None, :] % length) * (2.0 * np.pi / length)
    cos, sin = np.cos(angle), np.sin(angle)
    columns = []
    for first in (0, quarter):
        columns += [cos[:, first:first + quarter], -sin[:, first:first + quarter]]
    along = np.concatenate(columns, axis=1)
    along[:, quarter] = cos[:, half]
    parts = []
    for table in (along, cos, sin, along.T):
        high = table.astype(jnp.bfloat16)
        parts += [high, (table - high.astype(np.float64)).astype(jnp.bfloat16)]
    return np.stack(parts)


def halves(value):
    high = value.astype(jnp.bfloat16)
    return high, (value - high.astype(jnp.float32)).astype(jnp.bfloat16)


def dot(left, right):
    return jnp.dot(left, right, preferred_element_type=jnp.float32)


def dot3(left, right):
    return dot(left[0], right[0]) + (dot(left[0], right[1]) + dot(left[1], right[0]))


def kernel(
    dp_count, slab_count, voxel_count,
    rotation, weight_hbm, blocks_hbm, features_hbm, target_hbm, wedge_hbm, tables_hbm,
    out, out_sums,
    weight, blocks, features, target, wedge, tables, outgoing, plane, direct, cross, back, returned,
    late_table, spread_features, sums, own_sum, all_sums,
    load_sem, side_sem, send_sem, recv_sem, send2_sem, recv2_sem, sum_send_sem, sum_recv_sem,
):
    channels, depth, planes, length = features.shape
    pieces = depth // ROWS
    half, quarter = length // 2, length // 4
    my_dp, me = lax.axis_index("dp"), lax.axis_index("slab")
    slab_steps = range(slab_count - 1, 0, -1)

    def slab_peer(step):
        return lax.bitwise_xor(me, jnp.int32(step))

    def dp_peer(step):
        return lax.rem(my_dp + step, dp_count)

    loads = []
    for j in range(pieces):
        rows = pl.ds(j * ROWS, ROWS)
        loads.append(pltpu.make_async_copy(features_hbm.at[:, rows], features.at[:, rows], load_sem.at[j]))
    sides = [
        pltpu.make_async_copy(weight_hbm, weight, side_sem.at[0]),
        pltpu.make_async_copy(target_hbm, target, side_sem.at[1]),
        pltpu.make_async_copy(tables_hbm.at[0:2], tables.at[0:2], side_sem.at[2]),
        pltpu.make_async_copy(blocks_hbm, blocks, side_sem.at[3]),
        pltpu.make_async_copy(wedge_hbm, wedge, side_sem.at[4]),
        pltpu.make_async_copy(tables_hbm.at[2:8], tables.at[2:8], side_sem.at[5]),
    ]
    barrier = pltpu.get_barrier_semaphore()
    for r in slab_steps:
        pl.semaphore_signal(barrier, inc=1, device_id=(my_dp, slab_peer(r)), device_id_type=MESH)
    for r in range(1, dp_count):
        pl.semaphore_signal(barrier, inc=1, device_id=(dp_peer(r), me), device_id_type=MESH)
    for copy in (*sides[:2], loads[0], sides[2], *loads[1:], *sides[3:]):
        copy.start()

    def table(k):
        return tables[2 * k], tables[2 * k + 1]

    arrivals, departures = {}, []

    def all_but_one(ref, sem, *index):
        part = ref.at[index[0], pl.ds(0, slab_count - 1), index[1]]
        return pltpu.make_async_copy(part, part, sem)

    def exchange(kind, h, first, count, source, landing, sends, recvs):
        group = len([key for key in arrivals if key[0] == kind])
        rows = pl.ds(first * ROWS, count * ROWS)
        for r in slab_steps:
            peer = slab_peer(r)
            pltpu.make_async_remote_copy(
                src_ref=source.at[h, peer, rows],
                dst_ref=landing.at[h, me, rows],
                send_sem=sends.at[group],
                recv_sem=recvs.at[group],
                device_id=(my_dp, peer),
                device_id_type=MESH,
            ).start()
        arrivals[kind, h, first] = all_but_one(landing, recvs.at[group], h, rows)
        departures.append(all_but_one(source, sends.at[group], h, rows))

    for j in range(pieces):
        base = j * ROWS
        if j == 0:
            sides[0].wait()
            sides[1].wait()
        loads[j].wait()

        def add_channel(c, accs):
            scale = weight[c]
            return tuple(
                accs[z] + scale * features[c, base + z].astype(jnp.float32) for z in range(ROWS)
            )

        start = tuple(-target[base + z].astype(jnp.float32) for z in range(ROWS))
        accs = lax.fori_loop(0, channels, add_channel, start, unroll=4)
        if j == 0:
            sides[2].wait()
        lines = dot3(halves(jnp.concatenate(accs, axis=0)), table(0))
        lines = jnp.swapaxes(lines.reshape(ROWS, planes, length), 0, 1)
        for h in range(2):
            outgoing[h, :, pl.ds(base, ROWS), :] = lines[:, :, h * half:(h + 1) * half]
            plane[h, me, pl.ds(base, ROWS), :] = outgoing[h, me, pl.ds(base, ROWS), :]
        if j < HELD - 1:
            continue
        first = j
        if j == HELD - 1:
            pl.semaphore_wait(barrier, slab_count + dp_count - 2)
            first = 0
        exchange("out", 0, first, j + 1 - first, outgoing, plane, send_sem, recv_sem)
    for first in range(0, pieces, OUT_GROUP):
        exchange("out", 1, first, OUT_GROUP, outgoing, plane, send_sem, recv_sem)

    def transform_channels(first, groups):
        def transform(i, carry):
            for u in range(AT_ONCE):
                c = (first + i) * AT_ONCE + u
                rows = features[c].reshape(depth * planes, length)
                lines = dot(rows, late_table[...])
                spread_features[c] = (lines[:, :half] + lines[:, half:]).reshape(depth, planes, half)
            return carry

        lax.fori_loop(0, groups, transform, 0)

    late_table[:, :half] = tables[0, :, half:]
    late_table[:, half:] = tables[1, :, half:]
    sides[3].wait()
    sides[4].wait()
    row = lax.broadcasted_iota(jnp.int32, (length, length), 0)
    column = lax.broadcasted_iota(jnp.int32, (length, length), 1)
    row_block, column_block = row // BLK, column // BLK
    listed = jnp.zeros((length, length), jnp.bool_)
    for n in range(blocks.shape[1]):
        listed = listed | ((row_block == blocks[0, n]) & (column_block == blocks[1, n]))
    mask = jnp.where(listed, wedge[...], 0).astype(jnp.float32)
    mirror = jnp.where(lax.rem(row + column, length) == 0, 1.0, 0.0).astype(jnp.bfloat16)
    flipped = dot(dot(mirror, mask.astype(jnp.bfloat16)).astype(jnp.bfloat16), mirror)
    even = mask + flipped
    odd = lax.dot_general(
        even.astype(jnp.bfloat16), mirror, (((0,), (0,)), ((), ())), preferred_element_type=jnp.float32
    )
    is_odd = lax.rem(rotation[0], 2) == 1
    kept = jnp.where(is_odd, odd, even).astype(jnp.bfloat16)
    within = lax.rem(column, half)
    alone = lax.rem(column, quarter) + column // half == 0
    lane_freq = jnp.where(column == quarter, half, lax.rem(within, quarter) + column // half * quarter)
    spread = dot(kept, jnp.where(row == lane_freq, 1.0, 0.0).astype(jnp.bfloat16))
    scale = 1.0 / (length * length)
    direct[...] = spread * jnp.where(alone, scale, 2.0 * scale)
    cross[...] = spread * jnp.where(alone, 0.0, jnp.where(within < quarter, 2.0 * scale, -2.0 * scale))
    sides[5].wait()
    transform_channels(0, SPREAD[0])

    for h in range(2):
        for key in [key for key in arrivals if key[:2] == ("out", h)]:
            arrivals[key].wait()
        lines = halves(plane[h].reshape(length, half))
        even_part, odd_part = dot3(table(1), lines), dot3(table(2), lines)
        own, other = direct[:, h * half:(h + 1) * half], cross[:, h * half:(h + 1) * half]
        first = halves(own * even_part + other * pltpu.roll(odd_part, quarter, 1))
        second = halves(own * odd_part - other * pltpu.roll(even_part, quarter, 1))
        back[h] = (dot3(table(1), first) + dot3(table(2), second)).reshape(slab_count, depth, half)
        step = BACK_GROUPS[h]
        for j in range(0, pieces, step):
            exchange("back", h, j, step, back, returned, send2_sem, recv2_sem)
        returned[h, me] = back[h, me]
        transform_channels(sum(SPREAD[:h + 1]), SPREAD[h + 1])

    def inverse_rows(h):
        return tuple(part[h * half:(h + 1) * half] for part in table(3))

    for key in [key for key in arrivals if key[:2] == ("back", 0)]:
        arrivals[key].wait()
    lines = jnp.swapaxes(returned[0], 0, 1).reshape(depth * planes, half)
    out[...] = dot3(halves(lines), inverse_rows(0)).reshape(depth, planes, length)
    for j in range(pieces):
        grads = [out[j * ROWS + z] for z in range(ROWS)]

        def early_sums(i, carry):
            first = i * SUMMED
            accs = [grads[0] * features[first + u, j * ROWS].astype(jnp.float32) for u in range(SUMMED)]
            for z in range(1, ROWS):
                accs = [
                    accs[u] + grads[z] * features[first + u, j * ROWS + z].astype(jnp.float32) for u in range(SUMMED)
                ]
            for u in range(SUMMED):
                folded = accs[u][:, :half] + accs[u][:, half:]
                sums[first + u] = folded if j == 0 else sums[first + u] + folded
            return carry

        lax.fori_loop(0, channels // SUMMED, early_sums, 0)

    for j in range(pieces):
        base = j * ROWS
        if ("back", 1, j) in arrivals:
            arrivals["back", 1, j].wait()
        lines = jnp.swapaxes(returned[1, :, pl.ds(base, ROWS), :], 0, 1)

        def late_sums(i, carry):
            first = i * SUMMED
            accs = [lines[0] * spread_features[first + u, base] for u in range(SUMMED)]
            for z in range(1, ROWS):
                accs = [accs[u] + lines[z] * spread_features[first + u, base + z] for u in range(SUMMED)]
            for u in range(SUMMED):
                sums[first + u] = sums[first + u] + accs[u]
            return carry

        lax.fori_loop(0, channels // SUMMED, late_sums, 0)

    rest = jnp.sum(sums[...], axis=1)
    ones = jnp.ones((8, 128), jnp.bfloat16)
    row_sum = jnp.zeros((8, channels), jnp.float32)
    for _ in range(3):
        part = rest.astype(jnp.bfloat16)
        rest = rest - part.astype(jnp.float32)
        row_sum = row_sum + lax.dot_general(
            ones, part, (((1,), (1,)), ((), ())), preferred_element_type=jnp.float32
        )
    row_sum = row_sum[0:1]
    own_sum[0] = row_sum
    place = my_dp * slab_count + me
    for r in range(slab_count - 1, -1, -1):
        for k in range(dp_count - 1, -1, -1):
            if k == 0 and r == 0:
                continue
            pltpu.make_async_remote_copy(
                src_ref=own_sum.at[0],
                dst_ref=all_sums.at[place],
                send_sem=sum_send_sem.at[0],
                recv_sem=sum_recv_sem.at[0],
                device_id=(dp_peer(k), slab_peer(r)),
                device_id_type=MESH,
            ).start()
    all_sums[place] = row_sum
    lines = jnp.swapaxes(returned[1], 0, 1).reshape(depth * planes, half)
    out[...] = out[...] + dot3(halves(lines), inverse_rows(1)).reshape(depth, planes, length)
    for copy in departures:
        copy.wait()
    others = all_sums.at[pl.ds(0, dp_count * slab_count - 1)]
    pltpu.make_async_copy(others, others, sum_recv_sem.at[0]).wait()
    pltpu.make_async_copy(others, others, sum_send_sem.at[0]).wait()
    out_sums[...] = jnp.sum(all_sums[...], axis=0) / voxel_count


def hand_over(vol_grad, w_grad, out, out_weight_grad, sem):
    copies = [
        pltpu.make_async_copy(vol_grad, out, sem.at[0]),
        pltpu.make_async_copy(w_grad, out_weight_grad, sem.at[1]),
    ]
    for copy in copies:
        copy.start()
    for copy in copies:
        copy.wait()


def split_planes(features, target, out_weight, rotation, blocks, wedge):
    _, channels, depth, planes, length = features.shape
    dp_count, slab_count = lax.axis_size("dp"), lax.axis_size("slab")
    pieces = depth // ROWS
    half = length // 2
    voxel_count = dp_count * length * planes * length
    smem = pl.BlockSpec(memory_space=pltpu.SMEM)
    hbm = pl.BlockSpec(memory_space=pltpu.HBM)
    vmem = pl.BlockSpec(memory_space=pltpu.VMEM)
    dma = pltpu.SemaphoreType.DMA
    out_groups = pieces - HELD + 1 + pieces // OUT_GROUP
    back_groups = pieces // BACK_GROUPS[0] + pieces // BACK_GROUPS[1]
    vol_grad, w_grad = pl.pallas_call(
        functools.partial(kernel, dp_count, slab_count, float(voxel_count)),
        out_shape=(
            pltpu.VMEM((depth, planes, length), jnp.float32),
            pltpu.VMEM((1, channels), jnp.float32),
        ),
        in_specs=[smem, hbm, hbm, hbm, hbm, hbm, hbm],
        out_specs=(vmem, vmem),
        scratch_shapes=[
            pltpu.SMEM((channels,), jnp.float32),
            pltpu.SMEM((2, blocks.shape[0]), jnp.int32),
            pltpu.VMEM((channels, depth, planes, length), jnp.bfloat16),
            pltpu.VMEM((depth, planes, length), jnp.bfloat16),
            pltpu.VMEM((length, length), jnp.int32),
            pltpu.VMEM((8, length, length), jnp.bfloat16),
            pltpu.VMEM((2, planes, depth, half), jnp.float32),
            pltpu.VMEM((2, slab_count, depth, half), jnp.float32),
            pltpu.VMEM((length, length), jnp.float32),
            pltpu.VMEM((length, length), jnp.float32),
            pltpu.VMEM((2, slab_count, depth, half), jnp.float32),
            pltpu.VMEM((2, planes, depth, half), jnp.float32),
            pltpu.VMEM((length, length), jnp.bfloat16),
            pltpu.VMEM((channels, depth, planes, half), jnp.float32),
            pltpu.VMEM((channels, planes, half), jnp.float32),
            pltpu.VMEM((1, 1, channels), jnp.float32),
            pltpu.VMEM((dp_count * slab_count, 1, channels), jnp.float32),
            dma((pieces,)),
            dma((6,)),
            dma((out_groups,)),
            dma((out_groups,)),
            dma((back_groups,)),
            dma((back_groups,)),
            dma((1,)),
            dma((1,)),
        ],
        compiler_params=pltpu.CompilerParams(
            collective_id=0, has_side_effects=True, vmem_limit_bytes=56 * 1024 * 1024
        ),
    )(
        rotation, out_weight, blocks.T, features[0], target[0], wedge, jnp.asarray(fourier_tables(length)),
    )
    vol_grad, w_grad = pl.pallas_call(
        hand_over,
        out_shape=(
            jax.ShapeDtypeStruct(vol_grad.shape, jnp.float32),
            jax.ShapeDtypeStruct(w_grad.shape, jnp.float32),
        ),
        in_specs=[vmem, vmem],
        out_specs=(hbm, hbm),
        scratch_shapes=[dma((2,))],
    )(
        pltpu.with_memory_space_constraint(vol_grad, pltpu.VMEM),
        pltpu.with_memory_space_constraint(w_grad, pltpu.VMEM),
    )
    return vol_grad[None], w_grad[0]


def solution(mesh):
    def on_device(features, *rest):
        samples, _, depth, planes, length = features.shape
        whole_planes = (
            samples == 1
            and planes == 8
            and planes == mesh.shape["slab"]
            and depth % (4 * ROWS) == 0
            and length % 256 == 0
            and features.shape[1] % (AT_ONCE * sum(SPREAD)) == 0
        )
        return (split_planes if whole_planes else split_lines)(features, *rest)

    in_specs = (
        P("dp", None, "slab", None, None),
        P("dp", "slab", None, None),
        P(),
        P("dp"),
        P(),
        P(),
    )
    out_specs = (P("dp", "slab", None, None), P())
    return jax.shard_map(
        on_device, mesh=mesh, in_specs=in_specs, out_specs=out_specs, check_vma=False
    )
```

```python
import functools
import math

import numpy as np

import jax
import jax.numpy as jnp
from jax import lax
from jax.experimental import pallas as pl
from jax.experimental.pallas import tpu as pltpu
from jax.sharding import PartitionSpec as P

BLK = 64
ROWS = 8
OUT_GROUP = 2
HELD = 2
AT_ONCE = 8
SUMMED = 16
SPREAD = (5, 2, 1)
BACK_GROUPS = (4, 1)
MESH = pl.DeviceIdType.MESH


def product(form, left, right):
    return jnp.einsum(form, left, right, precision=lax.Precision.HIGHEST)


def wedge_weights(blocks, wedge, length):
    per_side = length // BLK
    labels = jnp.arange(per_side, dtype=jnp.int32)
    match = (blocks[:, 0][:, None, None] == labels[None, :, None]) & (
        blocks[:, 1][:, None, None] == labels[None, None, :]
    )
    listed = jnp.any(match, axis=0)
    spread = jnp.repeat(jnp.repeat(listed, BLK, axis=0), BLK, axis=1)
    return jnp.where(spread, wedge, 0).astype(jnp.float32)


def phase_tables(turns, length):
    positions = jnp.arange(length, dtype=jnp.int32)
    flip_depth = turns >= 2
    flip_width = (turns == 1) | (turns == 2)
    depth_index = jnp.where(
        flip_depth[:, None], length - 1 - positions[None, :], positions[None, :]
    )
    width_index = jnp.where(
        flip_width[:, None], length - 1 - positions[None, :], positions[None, :]
    )
    depth_phase = positions[None, :, None] * depth_index[:, None, :] % length
    width_phase = width_index[:, :, None] * positions[None, None, :] % length
    depth_angle = depth_phase.astype(jnp.float32) * (2.0 * math.pi / length)
    width_angle = width_phase.astype(jnp.float32) * (2.0 * math.pi / length)
    return (jnp.cos(depth_angle), jnp.sin(depth_angle), jnp.cos(width_angle), jnp.sin(width_angle))


def split_lines(features, target, out_weight, rotation, blocks, wedge):
    length = features.shape[-1]
    plane_count = features.shape[3]
    slab_count = lax.axis_size("slab")
    columns = length // slab_count
    col_start = lax.axis_index("slab") * columns
    features_wide = features.astype(jnp.float32)
    volume = product("c,sczyx->szyx", out_weight, features_wide)
    difference = volume - target.astype(jnp.float32)
    depth_cos, depth_sin, width_cos, width_sin = phase_tables(rotation, length)
    line_real = product("szyb,sbp->szyp", difference, width_cos)
    line_imag = -product("szyb,sbp->szyp", difference, width_sin)
    line_real, line_imag = (
        lax.all_to_all(line_real, "slab", split_axis=3, concat_axis=1, tiled=True),
        lax.all_to_all(line_imag, "slab", split_axis=3, concat_axis=1, tiled=True),
    )
    spec_real = (
        product("spa,sayq->spyq", depth_cos, line_real)
        + product("spa,sayq->spyq", depth_sin, line_imag)
    ) / length
    spec_imag = (
        product("spa,sayq->spyq", depth_cos, line_imag)
        - product("spa,sayq->spyq", depth_sin, line_real)
    ) / length
    mask = wedge_weights(blocks, wedge, length)
    odd_turn = rotation % 2 == 1
    mask_turned = jnp.where(odd_turn[:, None, None], mask.T[None], mask[None])
    mask_columns = lax.dynamic_slice_in_dim(mask_turned, col_start, columns, 2)
    grad_real = 2.0 * mask_columns[:, :, None, :] * spec_real
    grad_imag = 2.0 * mask_columns[:, :, None, :] * spec_imag
    back_real = product("spa,spyq->sayq", depth_cos, grad_real) - product(
        "spa,spyq->sayq", depth_sin, grad_imag
    )
    back_imag = product("spa,spyq->sayq", depth_cos, grad_imag) + product(
        "spa,spyq->sayq", depth_sin, grad_real
    )
    back_real, back_imag = (
        lax.all_to_all(back_real, "slab", split_axis=1, concat_axis=3, tiled=True),
        lax.all_to_all(back_imag, "slab", split_axis=1, concat_axis=3, tiled=True),
    )
    vol_grad = (
        product("sayp,sbp->sayb", back_real, width_cos)
        - product("sayp,sbp->sayb", back_imag, width_sin)
    ) / length
    voxel_count = lax.axis_size("dp") * features.shape[0] * length * plane_count * length
    local_sum = product("sczyx,szyx->c", features_wide, vol_grad) / voxel_count
    w_grad = lax.psum(local_sum, ("dp", "slab"))
    return (vol_grad, w_grad)


def fourier_tables(length):
    half, quarter = length // 2, length // 4
    index = np.arange(length)
    angle = (index[:, None] * index[None, :] % length) * (2.0 * np.pi / length)
    cos, sin = np.cos(angle), np.sin(angle)
    columns = []
    for first in (0, quarter):
        columns += [cos[:, first:first + quarter], -sin[:, first:first + quarter]]
    along = np.concatenate(columns, axis=1)
    along[:, quarter] = cos[:, half]
    parts = []
    for table in (along, cos, sin, along.T):
        high = table.astype(jnp.bfloat16)
        parts += [high, (table - high.astype(np.float64)).astype(jnp.bfloat16)]
    return np.stack(parts)


def halves(value):
    high = value.astype(jnp.bfloat16)
    return high, (value - high.astype(jnp.float32)).astype(jnp.bfloat16)


def dot(left, right):
    return jnp.dot(left, right, preferred_element_type=jnp.float32)


def dot3(left, right):
    return dot(left[0], right[0]) + (dot(left[0], right[1]) + dot(left[1], right[0]))


def kernel(
    dp_count, slab_count, voxel_count,
    rotation, weight_hbm, blocks_hbm, features_hbm, target_hbm, wedge_hbm, tables_hbm,
    out, out_sums,
    weight, blocks, features, target, wedge, tables, outgoing, plane, direct, cross, back, returned,
    late_table, spread_features, sums, own_sum, all_sums,
    load_sem, side_sem, send_sem, recv_sem, send2_sem, recv2_sem, sum_send_sem, sum_recv_sem,
):
    channels, depth, planes, length = features.shape
    pieces = depth // ROWS
    half, quarter = length // 2, length // 4
    my_dp, me = lax.axis_index("dp"), lax.axis_index("slab")
    slab_steps = range(slab_count - 1, 0, -1)

    def slab_peer(step):
        return lax.bitwise_xor(me, jnp.int32(step))

    def dp_peer(step):
        return lax.rem(my_dp + step, dp_count)

    loads = []
    for j in range(pieces):
        rows = pl.ds(j * ROWS, ROWS)
        loads.append(pltpu.make_async_copy(features_hbm.at[:, rows], features.at[:, rows], load_sem.at[j]))
    sides = [
        pltpu.make_async_copy(weight_hbm, weight, side_sem.at[0]),
        pltpu.make_async_copy(target_hbm, target, side_sem.at[1]),
        pltpu.make_async_copy(tables_hbm.at[0:2], tables.at[0:2], side_sem.at[2]),
        pltpu.make_async_copy(blocks_hbm, blocks, side_sem.at[3]),
        pltpu.make_async_copy(wedge_hbm, wedge, side_sem.at[4]),
        pltpu.make_async_copy(tables_hbm.at[2:8], tables.at[2:8], side_sem.at[5]),
    ]
    barrier = pltpu.get_barrier_semaphore()
    for r in slab_steps:
        pl.semaphore_signal(barrier, inc=1, device_id=(my_dp, slab_peer(r)), device_id_type=MESH)
    for r in range(1, dp_count):
        pl.semaphore_signal(barrier, inc=1, device_id=(dp_peer(r), me), device_id_type=MESH)
    for copy in (*sides[:2], loads[0], sides[2], *loads[1:], *sides[3:]):
        copy.start()

    def table(k):
        return tables[2 * k], tables[2 * k + 1]

    arrivals, departures = {}, []

    def all_but_one(ref, sem, *index):
        part = ref.at[index[0], pl.ds(0, slab_count - 1), index[1]]
        return pltpu.make_async_copy(part, part, sem)

    def exchange(kind, h, first, count, source, landing, sends, recvs):
        group = len([key for key in arrivals if key[0] == kind])
        rows = pl.ds(first * ROWS, count * ROWS)
        for r in slab_steps:
            peer = slab_peer(r)
            pltpu.make_async_remote_copy(
                src_ref=source.at[h, peer, rows],
                dst_ref=landing.at[h, me, rows],
                send_sem=sends.at[group],
                recv_sem=recvs.at[group],
                device_id=(my_dp, peer),
                device_id_type=MESH,
            ).start()
        arrivals[kind, h, first] = all_but_one(landing, recvs.at[group], h, rows)
        departures.append(all_but_one(source, sends.at[group], h, rows))

    for j in range(pieces):
        base = j * ROWS
        if j == 0:
            sides[0].wait()
            sides[1].wait()
        loads[j].wait()

        def add_channel(c, accs):
            scale = weight[c]
            return tuple(
                accs[z] + scale * features[c, base + z].astype(jnp.float32) for z in range(ROWS)
            )

        start = tuple(-target[base + z].astype(jnp.float32) for z in range(ROWS))
        accs = lax.fori_loop(0, channels, add_channel, start, unroll=4)
        if j == 0:
            sides[2].wait()
        lines = dot3(halves(jnp.concatenate(accs, axis=0)), table(0))
        lines = jnp.swapaxes(lines.reshape(ROWS, planes, length), 0, 1)
        for h in range(2):
            outgoing[h, :, pl.ds(base, ROWS), :] = lines[:, :, h * half:(h + 1) * half]
            plane[h, me, pl.ds(base, ROWS), :] = outgoing[h, me, pl.ds(base, ROWS), :]
        if j < HELD - 1:
            continue
        first = j
        if j == HELD - 1:
            pl.semaphore_wait(barrier, slab_count + dp_count - 2)
            first = 0
        exchange("out", 0, first, j + 1 - first, outgoing, plane, send_sem, recv_sem)
    for first in range(0, pieces, OUT_GROUP):
        exchange("out", 1, first, OUT_GROUP, outgoing, plane, send_sem, recv_sem)

    def transform_channels(first, groups):
        def transform(i, carry):
            for u in range(AT_ONCE):
                c = (first + i) * AT_ONCE + u
                rows = features[c].reshape(depth * planes, length)
                lines = dot(rows, late_table[...])
                spread_features[c] = (lines[:, :half] + lines[:, half:]).reshape(depth, planes, half)
            return carry

        lax.fori_loop(0, groups, transform, 0)

    late_table[:, :half] = tables[0, :, half:]
    late_table[:, half:] = tables[1, :, half:]
    sides[3].wait()
    sides[4].wait()
    row = lax.broadcasted_iota(jnp.int32, (length, length), 0)
    column = lax.broadcasted_iota(jnp.int32, (length, length), 1)
    row_block, column_block = row // BLK, column // BLK
    listed = jnp.zeros((length, length), jnp.bool_)
    for n in range(blocks.shape[1]):
        listed = listed | ((row_block == blocks[0, n]) & (column_block == blocks[1, n]))
    mask = jnp.where(listed, wedge[...], 0).astype(jnp.float32)
    mirror = jnp.where(lax.rem(row + column, length) == 0, 1.0, 0.0).astype(jnp.bfloat16)
    flipped = dot(dot(mirror, mask.astype(jnp.bfloat16)).astype(jnp.bfloat16), mirror)
    even = mask + flipped
    odd = lax.dot_general(
        even.astype(jnp.bfloat16), mirror, (((0,), (0,)), ((), ())), preferred_element_type=jnp.float32
    )
    is_odd = lax.rem(rotation[0], 2) == 1
    kept = jnp.where(is_odd, odd, even).astype(jnp.bfloat16)
    within = lax.rem(column, half)
    alone = lax.rem(column, quarter) + column // half == 0
    lane_freq = jnp.where(column == quarter, half, lax.rem(within, quarter) + column // half * quarter)
    spread = dot(kept, jnp.where(row == lane_freq, 1.0, 0.0).astype(jnp.bfloat16))
    scale = 1.0 / (length * length)
    direct[...] = spread * jnp.where(alone, scale, 2.0 * scale)
    cross[...] = spread * jnp.where(alone, 0.0, jnp.where(within < quarter, 2.0 * scale, -2.0 * scale))
    sides[5].wait()
    transform_channels(0, SPREAD[0])

    for h in range(2):
        for key in [key for key in arrivals if key[:2] == ("out", h)]:
            arrivals[key].wait()
        lines = halves(plane[h].reshape(length, half))
        even_part, odd_part = dot3(table(1), lines), dot3(table(2), lines)
        own, other = direct[:, h * half:(h + 1) * half], cross[:, h * half:(h + 1) * half]
        first = halves(own * even_part + other * pltpu.roll(odd_part, quarter, 1))
        second = halves(own * odd_part - other * pltpu.roll(even_part, quarter, 1))
        back[h] = (dot3(table(1), first) + dot3(table(2), second)).reshape(slab_count, depth, half)
        step = BACK_GROUPS[h]
        for j in range(0, pieces, step):
            exchange("back", h, j, step, back, returned, send2_sem, recv2_sem)
        returned[h, me] = back[h, me]
        transform_channels(sum(SPREAD[:h + 1]), SPREAD[h + 1])

    def inverse_rows(h):
        return tuple(part[h * half:(h + 1) * half] for part in table(3))

    for key in [key for key in arrivals if key[:2] == ("back", 0)]:
        arrivals[key].wait()
    lines = jnp.swapaxes(returned[0], 0, 1).reshape(depth * planes, half)
    out[...] = dot3(halves(lines), inverse_rows(0)).reshape(depth, planes, length)
    for j in range(pieces):
        grads = [out[j * ROWS + z] for z in range(ROWS)]

        def early_sums(i, carry):
            first = i * SUMMED
            accs = [grads[0] * features[first + u, j * ROWS].astype(jnp.float32) for u in range(SUMMED)]
            for z in range(1, ROWS):
                accs = [
                    accs[u] + grads[z] * features[first + u, j * ROWS + z].astype(jnp.float32) for u in range(SUMMED)
                ]
            for u in range(SUMMED):
                folded = accs[u][:, :half] + accs[u][:, half:]
                place = pl.ds(pl.multiple_of((first + u) * planes, planes), planes)
                sums[place] = folded if j == 0 else sums[place] + folded
            return carry

        lax.fori_loop(0, channels // SUMMED, early_sums, 0)

    for j in range(pieces):
        base = j * ROWS
        if ("back", 1, j) in arrivals:
            arrivals["back", 1, j].wait()
        lines = jnp.swapaxes(returned[1, :, pl.ds(base, ROWS), :], 0, 1)

        def late_sums(i, carry):
            first = i * SUMMED
            accs = [lines[0] * spread_features[first + u, base] for u in range(SUMMED)]
            for z in range(1, ROWS):
                accs = [accs[u] + lines[z] * spread_features[first + u, base + z] for u in range(SUMMED)]
            for u in range(SUMMED):
                place = pl.ds(pl.multiple_of((first + u) * planes, planes), planes)
                sums[place] = sums[place] + accs[u]
            return carry

        lax.fori_loop(0, channels // SUMMED, late_sums, 0)

    rest = sums[pl.ds(0, channels, stride=planes)]
    for y in range(1, planes):
        rest = rest + sums[pl.ds(y, channels, stride=planes)]
    ones = jnp.ones((8, 128), jnp.bfloat16)
    row_sum = jnp.zeros((8, channels), jnp.float32)
    for _ in range(3):
        part = rest.astype(jnp.bfloat16)
        rest = rest - part.astype(jnp.float32)
        row_sum = row_sum + lax.dot_general(
            ones, part, (((1,), (1,)), ((), ())), preferred_element_type=jnp.float32
        )
    row_sum = row_sum[0:1]
    own_sum[0] = row_sum
    place = my_dp * slab_count + me
    for r in range(slab_count - 1, -1, -1):
        for k in range(dp_count - 1, -1, -1):
            if k == 0 and r == 0:
                continue
            pltpu.make_async_remote_copy(
                src_ref=own_sum.at[0],
                dst_ref=all_sums.at[place],
                send_sem=sum_send_sem.at[0],
                recv_sem=sum_recv_sem.at[0],
                device_id=(dp_peer(k), slab_peer(r)),
                device_id_type=MESH,
            ).start()
    all_sums[place] = row_sum
    lines = jnp.swapaxes(returned[1], 0, 1).reshape(depth * planes, half)
    out[...] = out[...] + dot3(halves(lines), inverse_rows(1)).reshape(depth, planes, length)
    for copy in departures:
        copy.wait()
    others = all_sums.at[pl.ds(0, dp_count * slab_count - 1)]
    pltpu.make_async_copy(others, others, sum_recv_sem.at[0]).wait()
    pltpu.make_async_copy(others, others, sum_send_sem.at[0]).wait()
    out_sums[...] = jnp.sum(all_sums[...], axis=0) / voxel_count


def hand_over(vol_grad, w_grad, out, out_weight_grad, sem):
    copies = [
        pltpu.make_async_copy(vol_grad, out, sem.at[0]),
        pltpu.make_async_copy(w_grad, out_weight_grad, sem.at[1]),
    ]
    for copy in copies:
        copy.start()
    for copy in copies:
        copy.wait()


def split_planes(features, target, out_weight, rotation, blocks, wedge):
    _, channels, depth, planes, length = features.shape
    dp_count, slab_count = lax.axis_size("dp"), lax.axis_size("slab")
    pieces = depth // ROWS
    half = length // 2
    voxel_count = dp_count * length * planes * length
    smem = pl.BlockSpec(memory_space=pltpu.SMEM)
    hbm = pl.BlockSpec(memory_space=pltpu.HBM)
    vmem = pl.BlockSpec(memory_space=pltpu.VMEM)
    dma = pltpu.SemaphoreType.DMA
    out_groups = pieces - HELD + 1 + pieces // OUT_GROUP
    back_groups = pieces // BACK_GROUPS[0] + pieces // BACK_GROUPS[1]
    vol_grad, w_grad = pl.pallas_call(
        functools.partial(kernel, dp_count, slab_count, float(voxel_count)),
        out_shape=(
            pltpu.VMEM((depth, planes, length), jnp.float32),
            pltpu.VMEM((1, channels), jnp.float32),
        ),
        in_specs=[smem, hbm, hbm, hbm, hbm, hbm, hbm],
        out_specs=(vmem, vmem),
        scratch_shapes=[
            pltpu.SMEM((channels,), jnp.float32),
            pltpu.SMEM((2, blocks.shape[0]), jnp.int32),
            pltpu.VMEM((channels, depth, planes, length), jnp.bfloat16),
            pltpu.VMEM((depth, planes, length), jnp.bfloat16),
            pltpu.VMEM((length, length), jnp.int32),
            pltpu.VMEM((8, length, length), jnp.bfloat16),
            pltpu.VMEM((2, planes, depth, half), jnp.float32),
            pltpu.VMEM((2, slab_count, depth, half), jnp.float32),
            pltpu.VMEM((length, length), jnp.float32),
            pltpu.VMEM((length, length), jnp.float32),
            pltpu.VMEM((2, slab_count, depth, half), jnp.float32),
            pltpu.VMEM((2, planes, depth, half), jnp.float32),
            pltpu.VMEM((length, length), jnp.bfloat16),
            pltpu.VMEM((channels, depth, planes, half), jnp.float32),
            pltpu.VMEM((channels * planes, half), jnp.float32),
            pltpu.VMEM((1, 1, channels), jnp.float32),
            pltpu.VMEM((dp_count * slab_count, 1, channels), jnp.float32),
            dma((pieces,)),
            dma((6,)),
            dma((out_groups,)),
            dma((out_groups,)),
            dma((back_groups,)),
            dma((back_groups,)),
            dma((1,)),
            dma((1,)),
        ],
        compiler_params=pltpu.CompilerParams(
            collective_id=0, has_side_effects=True, vmem_limit_bytes=56 * 1024 * 1024
        ),
    )(
        rotation, out_weight, blocks.T, features[0], target[0], wedge, jnp.asarray(fourier_tables(length)),
    )
    vol_grad, w_grad = pl.pallas_call(
        hand_over,
        out_shape=(
            jax.ShapeDtypeStruct(vol_grad.shape, jnp.float32),
            jax.ShapeDtypeStruct(w_grad.shape, jnp.float32),
        ),
        in_specs=[vmem, vmem],
        out_specs=(hbm, hbm),
        scratch_shapes=[dma((2,))],
    )(
        pltpu.with_memory_space_constraint(vol_grad, pltpu.VMEM),
        pltpu.with_memory_space_constraint(w_grad, pltpu.VMEM),
    )
    return vol_grad[None], w_grad[0]


def solution(mesh):
    def on_device(features, *rest):
        samples, _, depth, planes, length = features.shape
        whole_planes = (
            samples == 1
            and planes == 8
            and planes == mesh.shape["slab"]
            and depth % (4 * ROWS) == 0
            and length % 256 == 0
            and features.shape[1] % (AT_ONCE * sum(SPREAD)) == 0
        )
        return (split_planes if whole_planes else split_lines)(features, *rest)

    in_specs = (
        P("dp", None, "slab", None, None),
        P("dp", "slab", None, None),
        P(),
        P("dp"),
        P(),
        P(),
    )
    out_specs = (P("dp", "slab", None, None), P())
    return jax.shard_map(
        on_device, mesh=mesh, in_specs=in_specs, out_specs=out_specs, check_vma=False
    )
```

```python
import functools
import math

import numpy as np

import jax
import jax.numpy as jnp
from jax import lax
from jax.experimental import pallas as pl
from jax.experimental.pallas import tpu as pltpu
from jax.sharding import PartitionSpec as P

BLK = 64
ROWS = 8
OUT_GROUP = 2
HELD = 2
AT_ONCE = 8
SUMMED = 16
SPREAD = (4, 2, 2)
BACK_GROUPS = (4, 2)
MESH = pl.DeviceIdType.MESH


def product(form, left, right):
    return jnp.einsum(form, left, right, precision=lax.Precision.HIGHEST)


def wedge_weights(blocks, wedge, length):
    per_side = length // BLK
    labels = jnp.arange(per_side, dtype=jnp.int32)
    match = (blocks[:, 0][:, None, None] == labels[None, :, None]) & (
        blocks[:, 1][:, None, None] == labels[None, None, :]
    )
    listed = jnp.any(match, axis=0)
    spread = jnp.repeat(jnp.repeat(listed, BLK, axis=0), BLK, axis=1)
    return jnp.where(spread, wedge, 0).astype(jnp.float32)


def phase_tables(turns, length):
    positions = jnp.arange(length, dtype=jnp.int32)
    flip_depth = turns >= 2
    flip_width = (turns == 1) | (turns == 2)
    depth_index = jnp.where(
        flip_depth[:, None], length - 1 - positions[None, :], positions[None, :]
    )
    width_index = jnp.where(
        flip_width[:, None], length - 1 - positions[None, :], positions[None, :]
    )
    depth_phase = positions[None, :, None] * depth_index[:, None, :] % length
    width_phase = width_index[:, :, None] * positions[None, None, :] % length
    depth_angle = depth_phase.astype(jnp.float32) * (2.0 * math.pi / length)
    width_angle = width_phase.astype(jnp.float32) * (2.0 * math.pi / length)
    return (jnp.cos(depth_angle), jnp.sin(depth_angle), jnp.cos(width_angle), jnp.sin(width_angle))


def split_lines(features, target, out_weight, rotation, blocks, wedge):
    length = features.shape[-1]
    plane_count = features.shape[3]
    slab_count = lax.axis_size("slab")
    columns = length // slab_count
    col_start = lax.axis_index("slab") * columns
    features_wide = features.astype(jnp.float32)
    volume = product("c,sczyx->szyx", out_weight, features_wide)
    difference = volume - target.astype(jnp.float32)
    depth_cos, depth_sin, width_cos, width_sin = phase_tables(rotation, length)
    line_real = product("szyb,sbp->szyp", difference, width_cos)
    line_imag = -product("szyb,sbp->szyp", difference, width_sin)
    line_real, line_imag = (
        lax.all_to_all(line_real, "slab", split_axis=3, concat_axis=1, tiled=True),
        lax.all_to_all(line_imag, "slab", split_axis=3, concat_axis=1, tiled=True),
    )
    spec_real = (
        product("spa,sayq->spyq", depth_cos, line_real)
        + product("spa,sayq->spyq", depth_sin, line_imag)
    ) / length
    spec_imag = (
        product("spa,sayq->spyq", depth_cos, line_imag)
        - product("spa,sayq->spyq", depth_sin, line_real)
    ) / length
    mask = wedge_weights(blocks, wedge, length)
    odd_turn = rotation % 2 == 1
    mask_turned = jnp.where(odd_turn[:, None, None], mask.T[None], mask[None])
    mask_columns = lax.dynamic_slice_in_dim(mask_turned, col_start, columns, 2)
    grad_real = 2.0 * mask_columns[:, :, None, :] * spec_real
    grad_imag = 2.0 * mask_columns[:, :, None, :] * spec_imag
    back_real = product("spa,spyq->sayq", depth_cos, grad_real) - product(
        "spa,spyq->sayq", depth_sin, grad_imag
    )
    back_imag = product("spa,spyq->sayq", depth_cos, grad_imag) + product(
        "spa,spyq->sayq", depth_sin, grad_real
    )
    back_real, back_imag = (
        lax.all_to_all(back_real, "slab", split_axis=1, concat_axis=3, tiled=True),
        lax.all_to_all(back_imag, "slab", split_axis=1, concat_axis=3, tiled=True),
    )
    vol_grad = (
        product("sayp,sbp->sayb", back_real, width_cos)
        - product("sayp,sbp->sayb", back_imag, width_sin)
    ) / length
    voxel_count = lax.axis_size("dp") * features.shape[0] * length * plane_count * length
    local_sum = product("sczyx,szyx->c", features_wide, vol_grad) / voxel_count
    w_grad = lax.psum(local_sum, ("dp", "slab"))
    return (vol_grad, w_grad)


def fourier_tables(length):
    half, quarter = length // 2, length // 4
    index = np.arange(length)
    angle = (index[:, None] * index[None, :] % length) * (2.0 * np.pi / length)
    cos, sin = np.cos(angle), np.sin(angle)
    columns = []
    for first in (0, quarter):
        columns += [cos[:, first:first + quarter], -sin[:, first:first + quarter]]
    along = np.concatenate(columns, axis=1)
    along[:, quarter] = cos[:, half]
    parts = []
    for table in (along, cos, sin, along.T):
        high = table.astype(jnp.bfloat16)
        parts += [high, (table - high.astype(np.float64)).astype(jnp.bfloat16)]
    return np.stack(parts)


def halves(value):
    high = value.astype(jnp.bfloat16)
    return high, (value - high.astype(jnp.float32)).astype(jnp.bfloat16)


def dot(left, right):
    return jnp.dot(left, right, preferred_element_type=jnp.float32)


def dot3(left, right):
    return dot(left[0], right[0]) + (dot(left[0], right[1]) + dot(left[1], right[0]))


def kernel(
    dp_count, slab_count, voxel_count,
    rotation, weight_hbm, blocks_hbm, features_hbm, target_hbm, wedge_hbm, tables_hbm,
    out, out_sums,
    weight, blocks, features, target, wedge, tables, outgoing, plane, direct, cross, back, returned,
    late_table, spread_features, sums, own_sum, all_sums,
    load_sem, side_sem, send_sem, recv_sem, send2_sem, recv2_sem, sum_send_sem, sum_recv_sem,
):
    channels, depth, planes, length = features.shape
    pieces = depth // ROWS
    half, quarter = length // 2, length // 4
    my_dp, me = lax.axis_index("dp"), lax.axis_index("slab")
    slab_steps = range(slab_count - 1, 0, -1)

    def slab_peer(step):
        return lax.bitwise_xor(me, jnp.int32(step))

    def dp_peer(step):
        return lax.rem(my_dp + step, dp_count)

    loads = []
    for j in range(pieces):
        rows = pl.ds(j * ROWS, ROWS)
        loads.append(pltpu.make_async_copy(features_hbm.at[:, rows], features.at[:, rows], load_sem.at[j]))
    sides = [
        pltpu.make_async_copy(weight_hbm, weight, side_sem.at[0]),
        pltpu.make_async_copy(target_hbm, target, side_sem.at[1]),
        pltpu.make_async_copy(tables_hbm.at[0:2], tables.at[0:2], side_sem.at[2]),
        pltpu.make_async_copy(blocks_hbm, blocks, side_sem.at[3]),
        pltpu.make_async_copy(wedge_hbm, wedge, side_sem.at[4]),
        pltpu.make_async_copy(tables_hbm.at[2:8], tables.at[2:8], side_sem.at[5]),
    ]
    barrier = pltpu.get_barrier_semaphore()
    for r in slab_steps:
        pl.semaphore_signal(barrier, inc=1, device_id=(my_dp, slab_peer(r)), device_id_type=MESH)
    for r in range(1, dp_count):
        pl.semaphore_signal(barrier, inc=1, device_id=(dp_peer(r), me), device_id_type=MESH)
    for copy in (*sides[:2], loads[0], sides[2], *loads[1:], *sides[3:]):
        copy.start()

    def table(k):
        return tables[2 * k], tables[2 * k + 1]

    arrivals, departures = {}, []

    def all_but_one(ref, sem, *index):
        part = ref.at[index[0], pl.ds(0, slab_count - 1), index[1]]
        return pltpu.make_async_copy(part, part, sem)

    def exchange(kind, h, first, count, source, landing, sends, recvs):
        group = len([key for key in arrivals if key[0] == kind])
        rows = pl.ds(first * ROWS, count * ROWS)
        for r in slab_steps:
            peer = slab_peer(r)
            pltpu.make_async_remote_copy(
                src_ref=source.at[h, peer, rows],
                dst_ref=landing.at[h, me, rows],
                send_sem=sends.at[group],
                recv_sem=recvs.at[group],
                device_id=(my_dp, peer),
                device_id_type=MESH,
            ).start()
        arrivals[kind, h, first] = all_but_one(landing, recvs.at[group], h, rows)
        departures.append(all_but_one(source, sends.at[group], h, rows))

    for j in range(pieces):
        base = j * ROWS
        if j == 0:
            sides[0].wait()
            sides[1].wait()
        loads[j].wait()

        def add_channel(c, accs):
            scale = weight[c]
            return tuple(
                accs[z] + scale * features[c, base + z].astype(jnp.float32) for z in range(ROWS)
            )

        start = tuple(-target[base + z].astype(jnp.float32) for z in range(ROWS))
        accs = lax.fori_loop(0, channels, add_channel, start, unroll=4)
        if j == 0:
            sides[2].wait()
        lines = dot3(halves(jnp.concatenate(accs, axis=0)), table(0))
        lines = jnp.swapaxes(lines.reshape(ROWS, planes, length), 0, 1)
        for h in range(2):
            outgoing[h, :, pl.ds(base, ROWS), :] = lines[:, :, h * half:(h + 1) * half]
            plane[h, me, pl.ds(base, ROWS), :] = outgoing[h, me, pl.ds(base, ROWS), :]
        if j < HELD - 1:
            continue
        first = j
        if j == HELD - 1:
            pl.semaphore_wait(barrier, slab_count + dp_count - 2)
            first = 0
        exchange("out", 0, first, j + 1 - first, outgoing, plane, send_sem, recv_sem)
    for first in range(0, pieces, OUT_GROUP):
        exchange("out", 1, first, OUT_GROUP, outgoing, plane, send_sem, recv_sem)

    def transform_channels(first, groups):
        def transform(i, carry):
            for u in range(AT_ONCE):
                c = (first + i) * AT_ONCE + u
                rows = features[c].reshape(depth * planes, length)
                lines = dot(rows, late_table[...])
                spread_features[c] = (lines[:, :half] + lines[:, half:]).reshape(depth, planes, half)
            return carry

        lax.fori_loop(0, groups, transform, 0)

    late_table[:, :half] = tables[0, :, half:]
    late_table[:, half:] = tables[1, :, half:]
    sides[3].wait()
    sides[4].wait()
    row = lax.broadcasted_iota(jnp.int32, (length, length), 0)
    column = lax.broadcasted_iota(jnp.int32, (length, length), 1)
    row_block, column_block = row // BLK, column // BLK
    listed = jnp.zeros((length, length), jnp.bool_)
    for n in range(blocks.shape[1]):
        listed = listed | ((row_block == blocks[0, n]) & (column_block == blocks[1, n]))
    mask = jnp.where(listed, wedge[...], 0).astype(jnp.float32)
    mirror = jnp.where(lax.rem(row + column, length) == 0, 1.0, 0.0).astype(jnp.bfloat16)
    flipped = dot(dot(mirror, mask.astype(jnp.bfloat16)).astype(jnp.bfloat16), mirror)
    even = mask + flipped
    odd = lax.dot_general(
        even.astype(jnp.bfloat16), mirror, (((0,), (0,)), ((), ())), preferred_element_type=jnp.float32
    )
    is_odd = lax.rem(rotation[0], 2) == 1
    kept = jnp.where(is_odd, odd, even).astype(jnp.bfloat16)
    within = lax.rem(column, half)
    alone = lax.rem(column, quarter) + column // half == 0
    lane_freq = jnp.where(column == quarter, half, lax.rem(within, quarter) + column // half * quarter)
    spread = dot(kept, jnp.where(row == lane_freq, 1.0, 0.0).astype(jnp.bfloat16))
    scale = 1.0 / (length * length)
    direct[...] = spread * jnp.where(alone, scale, 2.0 * scale)
    cross[...] = spread * jnp.where(alone, 0.0, jnp.where(within < quarter, 2.0 * scale, -2.0 * scale))
    sides[5].wait()
    transform_channels(0, SPREAD[0])

    for h in range(2):
        for key in [key for key in arrivals if key[:2] == ("out", h)]:
            arrivals[key].wait()
        lines = halves(plane[h].reshape(length, half))
        even_part, odd_part = dot3(table(1), lines), dot3(table(2), lines)
        own, other = direct[:, h * half:(h + 1) * half], cross[:, h * half:(h + 1) * half]
        first = halves(own * even_part + other * pltpu.roll(odd_part, quarter, 1))
        second = halves(own * odd_part - other * pltpu.roll(even_part, quarter, 1))
        back[h] = (dot3(table(1), first) + dot3(table(2), second)).reshape(slab_count, depth, half)
        step = BACK_GROUPS[h]
        for j in range(0, pieces, step):
            exchange("back", h, j, step, back, returned, send2_sem, recv2_sem)
        returned[h, me] = back[h, me]
        transform_channels(sum(SPREAD[:h + 1]), SPREAD[h + 1])

    def inverse_rows(h):
        return tuple(part[h * half:(h + 1) * half] for part in table(3))

    for key in [key for key in arrivals if key[:2] == ("back", 0)]:
        arrivals[key].wait()
    lines = jnp.swapaxes(returned[0], 0, 1).reshape(depth * planes, half)
    out[...] = dot3(halves(lines), inverse_rows(0)).reshape(depth, planes, length)
    for j in range(pieces):
        grads = [out[j * ROWS + z] for z in range(ROWS)]

        def early_sums(i, carry):
            first = i * SUMMED
            accs = [grads[0] * features[first + u, j * ROWS].astype(jnp.float32) for u in range(SUMMED)]
            for z in range(1, ROWS):
                accs = [
                    accs[u] + grads[z] * features[first + u, j * ROWS + z].astype(jnp.float32) for u in range(SUMMED)
                ]
            for u in range(SUMMED):
                folded = accs[u][:, :half] + accs[u][:, half:]
                place = pl.ds(pl.multiple_of((first + u) * planes, planes), planes)
                sums[place] = folded if j == 0 else sums[place] + folded
            return carry

        lax.fori_loop(0, channels // SUMMED, early_sums, 0)

    for j in range(pieces):
        base = j * ROWS
        if ("back", 1, j) in arrivals:
            arrivals["back", 1, j].wait()
        lines = jnp.swapaxes(returned[1, :, pl.ds(base, ROWS), :], 0, 1)

        def late_sums(i, carry):
            first = i * SUMMED
            accs = [lines[0] * spread_features[first + u, base] for u in range(SUMMED)]
            for z in range(1, ROWS):
                accs = [accs[u] + lines[z] * spread_features[first + u, base + z] for u in range(SUMMED)]
            for u in range(SUMMED):
                place = pl.ds(pl.multiple_of((first + u) * planes, planes), planes)
                sums[place] = sums[place] + accs[u]
            return carry

        lax.fori_loop(0, channels // SUMMED, late_sums, 0)

    rest = sums[pl.ds(0, channels, stride=planes)]
    for y in range(1, planes):
        rest = rest + sums[pl.ds(y, channels, stride=planes)]
    ones = jnp.ones((8, 128), jnp.bfloat16)
    row_sum = jnp.zeros((8, channels), jnp.float32)
    for _ in range(3):
        part = rest.astype(jnp.bfloat16)
        rest = rest - part.astype(jnp.float32)
        row_sum = row_sum + lax.dot_general(
            ones, part, (((1,), (1,)), ((), ())), preferred_element_type=jnp.float32
        )
    row_sum = row_sum[0:1]
    own_sum[0] = row_sum
    place = my_dp * slab_count + me
    for r in range(slab_count - 1, -1, -1):
        for k in range(dp_count - 1, -1, -1):
            if k == 0 and r == 0:
                continue
            pltpu.make_async_remote_copy(
                src_ref=own_sum.at[0],
                dst_ref=all_sums.at[place],
                send_sem=sum_send_sem.at[0],
                recv_sem=sum_recv_sem.at[0],
                device_id=(dp_peer(k), slab_peer(r)),
                device_id_type=MESH,
            ).start()
    all_sums[place] = row_sum
    lines = jnp.swapaxes(returned[1], 0, 1).reshape(depth * planes, half)
    out[...] = out[...] + dot3(halves(lines), inverse_rows(1)).reshape(depth, planes, length)
    for copy in departures:
        copy.wait()
    others = all_sums.at[pl.ds(0, dp_count * slab_count - 1)]
    pltpu.make_async_copy(others, others, sum_recv_sem.at[0]).wait()
    pltpu.make_async_copy(others, others, sum_send_sem.at[0]).wait()
    out_sums[...] = jnp.sum(all_sums[...], axis=0) / voxel_count


def hand_over(vol_grad, w_grad, out, out_weight_grad, sem):
    copies = [
        pltpu.make_async_copy(vol_grad, out, sem.at[0]),
        pltpu.make_async_copy(w_grad, out_weight_grad, sem.at[1]),
    ]
    for copy in copies:
        copy.start()
    for copy in copies:
        copy.wait()


def split_planes(features, target, out_weight, rotation, blocks, wedge):
    _, channels, depth, planes, length = features.shape
    dp_count, slab_count = lax.axis_size("dp"), lax.axis_size("slab")
    pieces = depth // ROWS
    half = length // 2
    voxel_count = dp_count * length * planes * length
    smem = pl.BlockSpec(memory_space=pltpu.SMEM)
    hbm = pl.BlockSpec(memory_space=pltpu.HBM)
    vmem = pl.BlockSpec(memory_space=pltpu.VMEM)
    dma = pltpu.SemaphoreType.DMA
    out_groups = pieces - HELD + 1 + pieces // OUT_GROUP
    back_groups = pieces // BACK_GROUPS[0] + pieces // BACK_GROUPS[1]
    vol_grad, w_grad = pl.pallas_call(
        functools.partial(kernel, dp_count, slab_count, float(voxel_count)),
        out_shape=(
            pltpu.VMEM((depth, planes, length), jnp.float32),
            pltpu.VMEM((1, channels), jnp.float32),
        ),
        in_specs=[smem, hbm, hbm, hbm, hbm, hbm, hbm],
        out_specs=(vmem, vmem),
        scratch_shapes=[
            pltpu.SMEM((channels,), jnp.float32),
            pltpu.SMEM((2, blocks.shape[0]), jnp.int32),
            pltpu.VMEM((channels, depth, planes, length), jnp.bfloat16),
            pltpu.VMEM((depth, planes, length), jnp.bfloat16),
            pltpu.VMEM((length, length), jnp.int32),
            pltpu.VMEM((8, length, length), jnp.bfloat16),
            pltpu.VMEM((2, planes, depth, half), jnp.float32),
            pltpu.VMEM((2, slab_count, depth, half), jnp.float32),
            pltpu.VMEM((length, length), jnp.float32),
            pltpu.VMEM((length, length), jnp.float32),
            pltpu.VMEM((2, slab_count, depth, half), jnp.float32),
            pltpu.VMEM((2, planes, depth, half), jnp.float32),
            pltpu.VMEM((length, length), jnp.bfloat16),
            pltpu.VMEM((channels, depth, planes, half), jnp.float32),
            pltpu.VMEM((channels * planes, half), jnp.float32),
            pltpu.VMEM((1, 1, channels), jnp.float32),
            pltpu.VMEM((dp_count * slab_count, 1, channels), jnp.float32),
            dma((pieces,)),
            dma((6,)),
            dma((out_groups,)),
            dma((out_groups,)),
            dma((back_groups,)),
            dma((back_groups,)),
            dma((1,)),
            dma((1,)),
        ],
        compiler_params=pltpu.CompilerParams(
            collective_id=0, has_side_effects=True, vmem_limit_bytes=56 * 1024 * 1024
        ),
    )(
        rotation, out_weight, blocks.T, features[0], target[0], wedge, jnp.asarray(fourier_tables(length)),
    )
    vol_grad, w_grad = pl.pallas_call(
        hand_over,
        out_shape=(
            jax.ShapeDtypeStruct(vol_grad.shape, jnp.float32),
            jax.ShapeDtypeStruct(w_grad.shape, jnp.float32),
        ),
        in_specs=[vmem, vmem],
        out_specs=(hbm, hbm),
        scratch_shapes=[dma((2,))],
    )(
        pltpu.with_memory_space_constraint(vol_grad, pltpu.VMEM),
        pltpu.with_memory_space_constraint(w_grad, pltpu.VMEM),
    )
    return vol_grad[None], w_grad[0]


def solution(mesh):
    def on_device(features, *rest):
        samples, _, depth, planes, length = features.shape
        whole_planes = (
            samples == 1
            and planes == 8
            and planes == mesh.shape["slab"]
            and depth % (4 * ROWS) == 0
            and length % 256 == 0
            and features.shape[1] % (AT_ONCE * sum(SPREAD)) == 0
        )
        return (split_planes if whole_planes else split_lines)(features, *rest)

    in_specs = (
        P("dp", None, "slab", None, None),
        P("dp", "slab", None, None),
        P(),
        P("dp"),
        P(),
        P(),
    )
    out_specs = (P("dp", "slab", None, None), P())
    return jax.shard_map(
        on_device, mesh=mesh, in_specs=in_specs, out_specs=out_specs, check_vma=False
    )
```

```python
import functools
import math

import numpy as np

import jax
import jax.numpy as jnp
from jax import lax
from jax.experimental import pallas as pl
from jax.experimental.pallas import tpu as pltpu
from jax.sharding import PartitionSpec as P

BLK = 64
ROWS = 8
OUT_GROUP = 2
HELD = 2
AT_ONCE = 8
SUMMED = 16
SPREAD = (5, 2, 1)
BACK_GROUPS = (4, 1)
MESH = pl.DeviceIdType.MESH


def product(form, left, right):
    return jnp.einsum(form, left, right, precision=lax.Precision.HIGHEST)


def wedge_weights(blocks, wedge, length):
    per_side = length // BLK
    labels = jnp.arange(per_side, dtype=jnp.int32)
    match = (blocks[:, 0][:, None, None] == labels[None, :, None]) & (
        blocks[:, 1][:, None, None] == labels[None, None, :]
    )
    listed = jnp.any(match, axis=0)
    spread = jnp.repeat(jnp.repeat(listed, BLK, axis=0), BLK, axis=1)
    return jnp.where(spread, wedge, 0).astype(jnp.float32)


def phase_tables(turns, length):
    positions = jnp.arange(length, dtype=jnp.int32)
    flip_depth = turns >= 2
    flip_width = (turns == 1) | (turns == 2)
    depth_index = jnp.where(
        flip_depth[:, None], length - 1 - positions[None, :], positions[None, :]
    )
    width_index = jnp.where(
        flip_width[:, None], length - 1 - positions[None, :], positions[None, :]
    )
    depth_phase = positions[None, :, None] * depth_index[:, None, :] % length
    width_phase = width_index[:, :, None] * positions[None, None, :] % length
    depth_angle = depth_phase.astype(jnp.float32) * (2.0 * math.pi / length)
    width_angle = width_phase.astype(jnp.float32) * (2.0 * math.pi / length)
    return (jnp.cos(depth_angle), jnp.sin(depth_angle), jnp.cos(width_angle), jnp.sin(width_angle))


def split_lines(features, target, out_weight, rotation, blocks, wedge):
    length = features.shape[-1]
    plane_count = features.shape[3]
    slab_count = lax.axis_size("slab")
    columns = length // slab_count
    col_start = lax.axis_index("slab") * columns
    features_wide = features.astype(jnp.float32)
    volume = product("c,sczyx->szyx", out_weight, features_wide)
    difference = volume - target.astype(jnp.float32)
    depth_cos, depth_sin, width_cos, width_sin = phase_tables(rotation, length)
    line_real = product("szyb,sbp->szyp", difference, width_cos)
    line_imag = -product("szyb,sbp->szyp", difference, width_sin)
    line_real, line_imag = (
        lax.all_to_all(line_real, "slab", split_axis=3, concat_axis=1, tiled=True),
        lax.all_to_all(line_imag, "slab", split_axis=3, concat_axis=1, tiled=True),
    )
    spec_real = (
        product("spa,sayq->spyq", depth_cos, line_real)
        + product("spa,sayq->spyq", depth_sin, line_imag)
    ) / length
    spec_imag = (
        product("spa,sayq->spyq", depth_cos, line_imag)
        - product("spa,sayq->spyq", depth_sin, line_real)
    ) / length
    mask = wedge_weights(blocks, wedge, length)
    odd_turn = rotation % 2 == 1
    mask_turned = jnp.where(odd_turn[:, None, None], mask.T[None], mask[None])
    mask_columns = lax.dynamic_slice_in_dim(mask_turned, col_start, columns, 2)
    grad_real = 2.0 * mask_columns[:, :, None, :] * spec_real
    grad_imag = 2.0 * mask_columns[:, :, None, :] * spec_imag
    back_real = product("spa,spyq->sayq", depth_cos, grad_real) - product(
        "spa,spyq->sayq", depth_sin, grad_imag
    )
    back_imag = product("spa,spyq->sayq", depth_cos, grad_imag) + product(
        "spa,spyq->sayq", depth_sin, grad_real
    )
    back_real, back_imag = (
        lax.all_to_all(back_real, "slab", split_axis=1, concat_axis=3, tiled=True),
        lax.all_to_all(back_imag, "slab", split_axis=1, concat_axis=3, tiled=True),
    )
    vol_grad = (
        product("sayp,sbp->sayb", back_real, width_cos)
        - product("sayp,sbp->sayb", back_imag, width_sin)
    ) / length
    voxel_count = lax.axis_size("dp") * features.shape[0] * length * plane_count * length
    local_sum = product("sczyx,szyx->c", features_wide, vol_grad) / voxel_count
    w_grad = lax.psum(local_sum, ("dp", "slab"))
    return (vol_grad, w_grad)


def fourier_tables(length):
    half, quarter = length // 2, length // 4
    index = np.arange(length)
    angle = (index[:, None] * index[None, :] % length) * (2.0 * np.pi / length)
    cos, sin = np.cos(angle), np.sin(angle)
    columns = []
    for first in (0, quarter):
        columns += [cos[:, first:first + quarter], -sin[:, first:first + quarter]]
    along = np.concatenate(columns, axis=1)
    along[:, quarter] = cos[:, half]
    parts = []
    for table in (along, cos, sin, along.T):
        high = table.astype(jnp.bfloat16)
        parts += [high, (table - high.astype(np.float64)).astype(jnp.bfloat16)]
    return np.stack(parts)


def halves(value):
    high = value.astype(jnp.bfloat16)
    return high, (value - high.astype(jnp.float32)).astype(jnp.bfloat16)


def dot(left, right):
    return jnp.dot(left, right, preferred_element_type=jnp.float32)


def dot3(left, right):
    return dot(left[0], right[0]) + (dot(left[0], right[1]) + dot(left[1], right[0]))


def kernel(
    dp_count, slab_count, voxel_count,
    rotation, weight_hbm, blocks_hbm, features_hbm, target_hbm, wedge_hbm, tables_hbm,
    out, out_sums,
    weight, blocks, features, target, wedge, tables, outgoing, plane, direct, cross, back, returned,
    late_table, spread_features, sums, own_sum, all_sums,
    load_sem, side_sem, send_sem, recv_sem, send2_sem, recv2_sem, sum_send_sem, sum_recv_sem,
):
    channels, depth, planes, length = features.shape
    pieces = depth // ROWS
    half, quarter = length // 2, length // 4
    my_dp, me = lax.axis_index("dp"), lax.axis_index("slab")
    slab_steps = range(slab_count - 1, 0, -1)

    def slab_peer(step):
        return lax.bitwise_xor(me, jnp.int32(step))

    def dp_peer(step):
        return lax.rem(my_dp + step, dp_count)

    loads = []
    for j in range(pieces):
        rows = pl.ds(j * ROWS, ROWS)
        loads.append(pltpu.make_async_copy(features_hbm.at[:, rows], features.at[:, rows], load_sem.at[j]))
    sides = [
        pltpu.make_async_copy(weight_hbm, weight, side_sem.at[0]),
        pltpu.make_async_copy(target_hbm, target, side_sem.at[1]),
        pltpu.make_async_copy(tables_hbm.at[0:2], tables.at[0:2], side_sem.at[2]),
        pltpu.make_async_copy(blocks_hbm, blocks, side_sem.at[3]),
        pltpu.make_async_copy(wedge_hbm, wedge, side_sem.at[4]),
        pltpu.make_async_copy(tables_hbm.at[2:8], tables.at[2:8], side_sem.at[5]),
    ]
    barrier = pltpu.get_barrier_semaphore()
    for r in slab_steps:
        pl.semaphore_signal(barrier, inc=1, device_id=(my_dp, slab_peer(r)), device_id_type=MESH)
    for r in range(1, dp_count):
        pl.semaphore_signal(barrier, inc=1, device_id=(dp_peer(r), me), device_id_type=MESH)
    for copy in (*sides[:2], loads[0], sides[2], *loads[1:], *sides[3:]):
        copy.start()

    def table(k):
        return tables[2 * k], tables[2 * k + 1]

    arrivals, departures = {}, []

    def all_but_one(ref, sem, *index):
        part = ref.at[index[0], pl.ds(0, slab_count - 1), index[1]]
        return pltpu.make_async_copy(part, part, sem)

    def exchange(kind, h, first, count, source, landing, sends, recvs):
        group = len([key for key in arrivals if key[0] == kind])
        rows = pl.ds(first * ROWS, count * ROWS)
        for r in slab_steps:
            peer = slab_peer(r)
            pltpu.make_async_remote_copy(
                src_ref=source.at[h, peer, rows],
                dst_ref=landing.at[h, me, rows],
                send_sem=sends.at[group],
                recv_sem=recvs.at[group],
                device_id=(my_dp, peer),
                device_id_type=MESH,
            ).start()
        arrivals[kind, h, first] = all_but_one(landing, recvs.at[group], h, rows)
        departures.append(all_but_one(source, sends.at[group], h, rows))

    for j in range(pieces):
        base = j * ROWS
        if j == 0:
            sides[0].wait()
            sides[1].wait()
        loads[j].wait()

        def add_channel(c, accs):
            scale = weight[c]
            return tuple(
                accs[z] + scale * features[c, base + z].astype(jnp.float32) for z in range(ROWS)
            )

        start = tuple(-target[base + z].astype(jnp.float32) for z in range(ROWS))
        accs = lax.fori_loop(0, channels, add_channel, start, unroll=4)
        if j == 0:
            sides[2].wait()
        lines = dot3(halves(jnp.concatenate(accs, axis=0)), table(0))
        lines = jnp.swapaxes(lines.reshape(ROWS, planes, length), 0, 1)
        for h in range(2):
            outgoing[h, :, pl.ds(base, ROWS), :] = lines[:, :, h * half:(h + 1) * half]
            plane[h, me, pl.ds(base, ROWS), :] = outgoing[h, me, pl.ds(base, ROWS), :]
        if j < HELD - 1:
            continue
        first = j
        if j == HELD - 1:
            pl.semaphore_wait(barrier, slab_count + dp_count - 2)
            first = 0
        exchange("out", 0, first, j + 1 - first, outgoing, plane, send_sem, recv_sem)
    exchange("out", 1, 0, OUT_GROUP, outgoing, plane, send_sem, recv_sem)

    def transform_channels(first, groups):
        def transform(i, carry):
            for u in range(AT_ONCE):
                c = (first + i) * AT_ONCE + u
                rows = features[c].reshape(depth * planes, length)
                lines = dot(rows, late_table[...])
                spread_features[c] = (lines[:, :half] + lines[:, half:]).reshape(depth, planes, half)
            return carry

        lax.fori_loop(0, groups, transform, 0)

    late_table[:, :half] = tables[0, :, half:]
    late_table[:, half:] = tables[1, :, half:]
    sides[3].wait()
    sides[4].wait()
    row = lax.broadcasted_iota(jnp.int32, (length, length), 0)
    column = lax.broadcasted_iota(jnp.int32, (length, length), 1)
    row_block, column_block = row // BLK, column // BLK
    listed = jnp.zeros((length, length), jnp.bool_)
    for n in range(blocks.shape[1]):
        listed = listed | ((row_block == blocks[0, n]) & (column_block == blocks[1, n]))
    mask = jnp.where(listed, wedge[...], 0).astype(jnp.float32)
    mirror = jnp.where(lax.rem(row + column, length) == 0, 1.0, 0.0).astype(jnp.bfloat16)
    flipped = dot(dot(mirror, mask.astype(jnp.bfloat16)).astype(jnp.bfloat16), mirror)
    even = mask + flipped
    odd = lax.dot_general(
        even.astype(jnp.bfloat16), mirror, (((0,), (0,)), ((), ())), preferred_element_type=jnp.float32
    )
    is_odd = lax.rem(rotation[0], 2) == 1
    kept = jnp.where(is_odd, odd, even).astype(jnp.bfloat16)
    within = lax.rem(column, half)
    alone = lax.rem(column, quarter) + column // half == 0
    lane_freq = jnp.where(column == quarter, half, lax.rem(within, quarter) + column // half * quarter)
    spread = dot(kept, jnp.where(row == lane_freq, 1.0, 0.0).astype(jnp.bfloat16))
    scale = 1.0 / (length * length)
    direct[...] = spread * jnp.where(alone, scale, 2.0 * scale)
    cross[...] = spread * jnp.where(alone, 0.0, jnp.where(within < quarter, 2.0 * scale, -2.0 * scale))
    sides[5].wait()
    for first in range(OUT_GROUP, pieces, OUT_GROUP):
        exchange("out", 1, first, OUT_GROUP, outgoing, plane, send_sem, recv_sem)
    transform_channels(0, SPREAD[0])

    for h in range(2):
        for key in [key for key in arrivals if key[:2] == ("out", h)]:
            arrivals[key].wait()
        lines = halves(plane[h].reshape(length, half))
        even_part, odd_part = dot3(table(1), lines), dot3(table(2), lines)
        own, other = direct[:, h * half:(h + 1) * half], cross[:, h * half:(h + 1) * half]
        first = halves(own * even_part + other * pltpu.roll(odd_part, quarter, 1))
        second = halves(own * odd_part - other * pltpu.roll(even_part, quarter, 1))
        back[h] = (dot3(table(1), first) + dot3(table(2), second)).reshape(slab_count, depth, half)
        step = BACK_GROUPS[h]
        for j in range(0, pieces, step):
            exchange("back", h, j, step, back, returned, send2_sem, recv2_sem)
        returned[h, me] = back[h, me]
        transform_channels(sum(SPREAD[:h + 1]), SPREAD[h + 1])

    def inverse_rows(h):
        return tuple(part[h * half:(h + 1) * half] for part in table(3))

    for key in [key for key in arrivals if key[:2] == ("back", 0)]:
        arrivals[key].wait()
    lines = jnp.swapaxes(returned[0], 0, 1).reshape(depth * planes, half)
    out[...] = dot3(halves(lines), inverse_rows(0)).reshape(depth, planes, length)
    for j in range(pieces):
        grads = [out[j * ROWS + z] for z in range(ROWS)]

        def early_sums(i, carry):
            first = i * SUMMED
            accs = [grads[0] * features[first + u, j * ROWS].astype(jnp.float32) for u in range(SUMMED)]
            for z in range(1, ROWS):
                accs = [
                    accs[u] + grads[z] * features[first + u, j * ROWS + z].astype(jnp.float32) for u in range(SUMMED)
                ]
            for u in range(SUMMED):
                folded = accs[u][:, :half] + accs[u][:, half:]
                place = pl.ds(pl.multiple_of((first + u) * planes, planes), planes)
                sums[place] = folded if j == 0 else sums[place] + folded
            return carry

        lax.fori_loop(0, channels // SUMMED, early_sums, 0)

    for j in range(pieces):
        base = j * ROWS
        if ("back", 1, j) in arrivals:
            arrivals["back", 1, j].wait()
        lines = jnp.swapaxes(returned[1, :, pl.ds(base, ROWS), :], 0, 1)

        def late_sums(i, carry):
            first = i * SUMMED
            accs = [lines[0] * spread_features[first + u, base] for u in range(SUMMED)]
            for z in range(1, ROWS):
                accs = [accs[u] + lines[z] * spread_features[first + u, base + z] for u in range(SUMMED)]
            for u in range(SUMMED):
                place = pl.ds(pl.multiple_of((first + u) * planes, planes), planes)
                sums[place] = sums[place] + accs[u]
            return carry

        lax.fori_loop(0, channels // SUMMED, late_sums, 0)

    rest = sums[pl.ds(0, channels, stride=planes)]
    for y in range(1, planes):
        rest = rest + sums[pl.ds(y, channels, stride=planes)]
    ones = jnp.ones((8, 128), jnp.bfloat16)
    row_sum = jnp.zeros((8, channels), jnp.float32)
    for _ in range(3):
        part = rest.astype(jnp.bfloat16)
        rest = rest - part.astype(jnp.float32)
        row_sum = row_sum + lax.dot_general(
            ones, part, (((1,), (1,)), ((), ())), preferred_element_type=jnp.float32
        )
    row_sum = row_sum[0:1]
    own_sum[0] = row_sum
    place = my_dp * slab_count + me
    for r in range(slab_count - 1, -1, -1):
        for k in range(dp_count - 1, -1, -1):
            if k == 0 and r == 0:
                continue
            pltpu.make_async_remote_copy(
                src_ref=own_sum.at[0],
                dst_ref=all_sums.at[place],
                send_sem=sum_send_sem.at[0],
                recv_sem=sum_recv_sem.at[0],
                device_id=(dp_peer(k), slab_peer(r)),
                device_id_type=MESH,
            ).start()
    all_sums[place] = row_sum
    lines = jnp.swapaxes(returned[1], 0, 1).reshape(depth * planes, half)
    out[...] = out[...] + dot3(halves(lines), inverse_rows(1)).reshape(depth, planes, length)
    for copy in departures:
        copy.wait()
    others = all_sums.at[pl.ds(0, dp_count * slab_count - 1)]
    pltpu.make_async_copy(others, others, sum_recv_sem.at[0]).wait()
    pltpu.make_async_copy(others, others, sum_send_sem.at[0]).wait()
    out_sums[...] = jnp.sum(all_sums[...], axis=0) / voxel_count


def hand_over(vol_grad, w_grad, out, out_weight_grad, sem):
    copies = [
        pltpu.make_async_copy(vol_grad, out, sem.at[0]),
        pltpu.make_async_copy(w_grad, out_weight_grad, sem.at[1]),
    ]
    for copy in copies:
        copy.start()
    for copy in copies:
        copy.wait()


def split_planes(features, target, out_weight, rotation, blocks, wedge):
    _, channels, depth, planes, length = features.shape
    dp_count, slab_count = lax.axis_size("dp"), lax.axis_size("slab")
    pieces = depth // ROWS
    half = length // 2
    voxel_count = dp_count * length * planes * length
    smem = pl.BlockSpec(memory_space=pltpu.SMEM)
    hbm = pl.BlockSpec(memory_space=pltpu.HBM)
    vmem = pl.BlockSpec(memory_space=pltpu.VMEM)
    dma = pltpu.SemaphoreType.DMA
    out_groups = pieces - HELD + 1 + pieces // OUT_GROUP
    back_groups = pieces // BACK_GROUPS[0] + pieces // BACK_GROUPS[1]
    vol_grad, w_grad = pl.pallas_call(
        functools.partial(kernel, dp_count, slab_count, float(voxel_count)),
        out_shape=(
            pltpu.VMEM((depth, planes, length), jnp.float32),
            pltpu.VMEM((1, channels), jnp.float32),
        ),
        in_specs=[smem, hbm, hbm, hbm, hbm, hbm, hbm],
        out_specs=(vmem, vmem),
        scratch_shapes=[
            pltpu.SMEM((channels,), jnp.float32),
            pltpu.SMEM((2, blocks.shape[0]), jnp.int32),
            pltpu.VMEM((channels, depth, planes, length), jnp.bfloat16),
            pltpu.VMEM((depth, planes, length), jnp.bfloat16),
            pltpu.VMEM((length, length), jnp.int32),
            pltpu.VMEM((8, length, length), jnp.bfloat16),
            pltpu.VMEM((2, planes, depth, half), jnp.float32),
            pltpu.VMEM((2, slab_count, depth, half), jnp.float32),
            pltpu.VMEM((length, length), jnp.float32),
            pltpu.VMEM((length, length), jnp.float32),
            pltpu.VMEM((2, slab_count, depth, half), jnp.float32),
            pltpu.VMEM((2, planes, depth, half), jnp.float32),
            pltpu.VMEM((length, length), jnp.bfloat16),
            pltpu.VMEM((channels, depth, planes, half), jnp.float32),
            pltpu.VMEM((channels * planes, half), jnp.float32),
            pltpu.VMEM((1, 1, channels), jnp.float32),
            pltpu.VMEM((dp_count * slab_count, 1, channels), jnp.float32),
            dma((pieces,)),
            dma((6,)),
            dma((out_groups,)),
            dma((out_groups,)),
            dma((back_groups,)),
            dma((back_groups,)),
            dma((1,)),
            dma((1,)),
        ],
        compiler_params=pltpu.CompilerParams(
            collective_id=0, has_side_effects=True, vmem_limit_bytes=56 * 1024 * 1024
        ),
    )(
        rotation, out_weight, blocks.T, features[0], target[0], wedge, jnp.asarray(fourier_tables(length)),
    )
    vol_grad, w_grad = pl.pallas_call(
        hand_over,
        out_shape=(
            jax.ShapeDtypeStruct(vol_grad.shape, jnp.float32),
            jax.ShapeDtypeStruct(w_grad.shape, jnp.float32),
        ),
        in_specs=[vmem, vmem],
        out_specs=(hbm, hbm),
        scratch_shapes=[dma((2,))],
    )(
        pltpu.with_memory_space_constraint(vol_grad, pltpu.VMEM),
        pltpu.with_memory_space_constraint(w_grad, pltpu.VMEM),
    )
    return vol_grad[None], w_grad[0]


def solution(mesh):
    def on_device(features, *rest):
        samples, _, depth, planes, length = features.shape
        whole_planes = (
            samples == 1
            and planes == 8
            and planes == mesh.shape["slab"]
            and depth % (4 * ROWS) == 0
            and length % 256 == 0
            and features.shape[1] % (AT_ONCE * sum(SPREAD)) == 0
        )
        return (split_planes if whole_planes else split_lines)(features, *rest)

    in_specs = (
        P("dp", None, "slab", None, None),
        P("dp", "slab", None, None),
        P(),
        P("dp"),
        P(),
        P(),
    )
    out_specs = (P("dp", "slab", None, None), P())
    return jax.shard_map(
        on_device, mesh=mesh, in_specs=in_specs, out_specs=out_specs, check_vma=False
    )
```
